128 devices in a mesh: gz: 8 (over z, core), xy: 16 (over y, x).
Axes of the slice: x: 4, y: 4, z: 4, core: 2. Of those that a mesh axis runs over, the one named last changes fastest.
Arguments:
- voltage: float32 [64, 16384], P('gz', 'xy'), may hold values from -0.5 to 1
- gates: float32 [40, 64, 16384], P(None, 'gz', 'xy'), may hold values from 0 to 1
- couple_x: float32 [64, 16384], P('gz', 'xy'), may hold values from 150 to 600
- couple_y: float32 [64, 16384], P('gz', 'xy'), may hold values from 0.05 to 0.3
- gate_half: float32 [40], replicated, may hold values from -0.8 to 0.8
- gate_slope: float32 [40], replicated, may hold values from -6 to 6
- gate_rate: float32 [40], replicated, may hold values from 0.02 to 2
- conductance: float32 [40], replicated, may hold values from 0.002 to 0.03
- reversal: float32 [40], replicated, may hold values from -1.5 to 1.5
- purk_volt: float32 [512, 128], P('xy'), may hold values from -0.2 to 1.1
- purk_recovery: float32 [512, 128], P('xy'), may hold values from 0 to 0.5
- purk_couple: float32 [512, 128], P('xy'), may hold values from 0.12 to 0.26
- parent: int32 [512], replicated, may hold values from -1 to 511, as said below
- junc_purk: int32 [4096], P('xy'), may hold values from 0 to 4095
- junc_cell: int32 [4096], P('xy'), may hold values from 0 to 8191
- junc_owner: int32 [4096, 1], P('xy'), may hold values from 0 to 127; in each aligned block of 256 rows (0 to 255, 256 to 511, ...) at most 4 rows name the same one
- junc_gain: float32 [4096], P('xy'), may hold values from 0.05 to 0.3
Outputs:
- membrane: float32 [64, 16384], P('gz', 'xy')
- gating: float32 [40, 64, 16384], P(None, 'gz', 'xy')
- purkinje: float32 [512, 128], P('xy')
- recovery: float32 [512, 128], P('xy')
The draws below stay inside these ranges and needn't reach their ends.
Inputs may be any that keep to these rules, and one draw needn't show every extreme that they name: `junc_owner`: among the 256 junctions of one index of xy no device owns more than 4; owner o is the device at gz index o // 16 and xy index o % 16. Subtree 512 - 1 is the root with parent -1; every other subtree's parent is another subtree, following parents from any subtree reaches the root, and no subtree has more than two children.
All inputs are finite; a program needn't handle non-finite values.
Results may differ from the reference program's by a relative error of at most 0.0003.
Values sent between devices are 32-bit elements; how exact they have to be, the bound alone decides.
No kernel may reach another device: no remote copies, remote signals or barrier semaphores. Data moves between devices by JAX's collectives and lax.ppermute only.
A program may use at most 64 MiB of HBM per device.

```python
import math
import jax
import jax.numpy as jnp
import numpy as np
from jax import lax

BX = 8
BY = 1024
VARS = 40
SUB_DEV = 32
SEG = 128
JUNC_DEV = 256
STEPS = 16
NX = 64
NY = 16384
SUBTREES = 512
JUNCTIONS = 4096
CAP = 4
N_XY = 16
DEVICES = 128


def heap_layout(key):
    shuffled = jax.random.permutation(jax.random.fold_in(key, 7), SUBTREES - 1).astype(jnp.int32)
    heap_order = jnp.concatenate([jnp.full((1,), SUBTREES - 1, jnp.int32), shuffled])
    return heap_order


def draw_parent(key, part):
    heap_order = heap_layout(key)
    position = jnp.arange(SUBTREES, dtype=jnp.int32)
    above_node = heap_order[jnp.maximum(position - 1, 0) // 2]
    above_node = jnp.where(position == 0, -1, above_node).astype(jnp.int32)
    return jnp.zeros((SUBTREES,), jnp.int32).at[heap_order].set(above_node)


def draw_purk_volt(key, part):
    heap_order = heap_layout(key)
    position_of = jnp.zeros((SUBTREES,), jnp.int32).at[heap_order].set(jnp.arange(SUBTREES, dtype=jnp.int32))
    powers_two = 2 ** jnp.arange(1, 31, dtype=jnp.int32)
    depth_level = jnp.sum((position_of[:, None] + 1 >= powers_two[None, :]).astype(jnp.int32), axis=1)
    end_volts = jnp.where(depth_level % 2 == 0, 1.1, -0.2).astype(jnp.float32)
    uniform_part = jax.random.uniform(jax.random.fold_in(key, 13), (SUBTREES, SEG), jnp.float32)
    interior = -0.2 + 1.3 * uniform_part
    node_place = jnp.arange(SEG, dtype=jnp.int32)
    is_end = jnp.logical_or(node_place == 0, node_place == SEG - 1)
    return jnp.where(is_end[None, :], end_volts[:, None], interior).astype(jnp.float32)


def draw_voltage(key, part):
    row_place = jnp.arange(NX, dtype=jnp.float32)[:, None]
    row_share = row_place / (NX - 1)
    reversed_ramp = jax.random.bernoulli(jax.random.fold_in(key, 11), 0.5, (1, NY))
    row_share = jnp.where(reversed_ramp, 1.0 - row_share, row_share)
    uniform_part = jax.random.uniform(jax.random.fold_in(key, 17), (NX, NY), jnp.float32)
    ramp_part = -0.5 + 1.5 * row_share
    rough_part = 0.9 * uniform_part - 0.45
    return jnp.clip(ramp_part + rough_part, -0.5, 1.0).astype(jnp.float32)


def with_ends(result, key, low, largest):
    dims = result.shape
    place = [jax.random.randint(jax.random.fold_in(key, axis), (), 0, dims[axis]) for axis in range(len(dims))]
    result = result.at[tuple(place)].set(low)
    longest = dims.index(max(dims))
    place[longest] = (place[longest] + 1) % dims[longest]
    return result.at[tuple(place)].set(largest)


def block_levels(rng, extent, split, least, high):
    def one(axis_at, parts):
        draws = jax.random.uniform(jax.random.fold_in(jax.random.fold_in(rng, 6), axis_at), (parts,), jnp.float32, least / len(split), high / len(split))
        return jnp.repeat(jnp.exp(draws), extent[axis_at] // parts).reshape((-1,) + (1,) * (len(extent) - axis_at - 1))

    level = one(*split[0])
    for cut in split[1:]:
        level = level * one(*cut)
    return level


def deal_out(stream_key, own, number, rows, amount, top, most, slope):
    sequence = jax.random.permutation(stream_key, amount)
    heavy_load, usual = portions_of(amount, rows * top, most, slope, True), portions_of(amount, rows * top, most, slope, False)
    places = jnp.arange(amount)

    def named(tallies, rotation):
        used = int((tallies > 0).sum())
        fixed = max(1, used // 4)
        passed = fixed + (places - fixed + rotation * (used - fixed)) % max(1, amount - fixed)
        return jnp.zeros((amount,), jnp.int32).at[sequence[jnp.where(places < fixed, places, passed)]].set(jnp.asarray(tallies, jnp.int32))

    tallies = jnp.where(number % 4 == 0, named(heavy_load, number // 4), named(usual, number - number // 4 - 1))
    mixed = jax.random.permutation(jax.random.fold_in(own, 3), amount)
    giver, taker = mixed[0:amount // 2 * 2:2], mixed[1:amount // 2 * 2:2]
    room = jnp.minimum(tallies[giver] - 1, most - tallies[taker]) // 2
    room = jnp.where((giver == sequence[0]) | (taker == sequence[0]) | (tallies[taker] == 0), 0, jnp.maximum(room, 0))
    passed = jax.random.randint(jax.random.fold_in(own, 4), (amount // 2,), 0, 1 << 20) % (room + 1)
    tallies = tallies.at[giver].add(-passed).at[taker].add(passed)
    items = jnp.searchsorted(jnp.cumsum(tallies), jnp.arange(rows * top), side="right").astype(jnp.int32)
    table = items.reshape(top, rows).T
    table = table[jax.random.permutation(jax.random.fold_in(own, 1), rows)]
    rotation = jax.random.randint(jax.random.fold_in(own, 2), (rows, 1), 0, top)
    return jnp.take_along_axis(table, (jnp.arange(top)[None, :] + rotation) % top, axis=1)


def portions_of(amount, total, limit, slope, full):
    portions = [(1 << 20) // math.isqrt(standing ** slope) + 1 for standing in range(1, amount + 1)]
    largest = limit if full else min(limit, max(-(-total // amount), total * portions[0] // sum(portions)))
    least = 1 if total - largest >= amount - 1 else 0
    given, spare = [largest] + [least] * (amount - 1), total - largest - least * (amount - 1)
    while spare > 0:
        movable = [i for i in range(1, amount) if given[i] < largest] or [i for i in range(1, amount) if given[i] < limit]
        whole, left = sum([portions[i] for i in movable]), spare
        for i in movable:
            addition = min(limit - given[i], max(1, left * portions[i] // whole), spare)
            given[i] = given[i] + addition
            spare = spare - addition
    return np.array(given)


def setup_inputs(seed: int = 0) -> dict:
    arg_keys = jax.random.split(jax.random.key(seed), 18)
    voltage = draw_voltage(jax.random.fold_in(arg_keys[17], 71), 0)
    gates = jnp.clip(1.0 * jax.random.uniform(arg_keys[1], (VARS, NX, NY), jnp.float32) ** block_levels(arg_keys[1], (VARS, NX, NY), ((1, 8), (2, 16)), -0.2, 0.2), 0.0, 1.0)
    couple_x = jnp.clip(jnp.exp(math.log(600.0) - 1.3862944 * jax.random.uniform(arg_keys[2], (NX, NY), jnp.float32) ** block_levels(arg_keys[2], (NX, NY), ((0, 8), (1, 16)), -0.2, 0.2)), 150.0, 600.0)
    couple_y = jnp.clip(0.05 + 0.25 * jax.random.uniform(arg_keys[3], (NX, NY), jnp.float32) ** block_levels(arg_keys[3], (NX, NY), ((0, 8), (1, 16)), -0.2, 0.2), 0.05, 0.3)
    gate_half = jnp.clip(jax.random.uniform(arg_keys[4], (VARS,), jnp.float32, -0.8, 0.8), -0.8, 0.8)
    gate_slope = jnp.clip(jax.random.uniform(arg_keys[5], (VARS,), jnp.float32, -6.0, 6.0), -6.0, 6.0)
    gate_rate = jnp.clip(jnp.exp(jax.random.uniform(arg_keys[6], (VARS,), jnp.float32, math.log(0.02), math.log(2.0))), 0.02, 2.0)
    conductance = jnp.clip(jnp.exp(jax.random.uniform(arg_keys[7], (VARS,), jnp.float32, math.log(0.002), math.log(0.03))), 0.002, 0.03)
    reversal = jnp.clip(jax.random.uniform(arg_keys[8], (VARS,), jnp.float32, -1.5, 1.5), -1.5, 1.5)
    purk_volt = draw_purk_volt(jax.random.fold_in(arg_keys[17], 71), 0)
    purk_recovery = jnp.clip(0.5 * jax.random.uniform(arg_keys[10], (SUBTREES, SEG), jnp.float32) ** block_levels(arg_keys[10], (SUBTREES, SEG), ((0, 16),), -0.2, 0.2), 0.0, 0.5)
    purk_couple = jnp.clip(jnp.exp(math.log(0.26) - 0.7731899 * jax.random.uniform(arg_keys[11], (SUBTREES, SEG), jnp.float32) ** block_levels(arg_keys[11], (SUBTREES, SEG), ((0, 16),), -0.2, 0.2)), 0.12, 0.26)
    parent = draw_parent(jax.random.fold_in(arg_keys[17], 71), 0)
    junc_purk = with_ends(jax.random.randint(arg_keys[13], (JUNCTIONS,), 0, SUB_DEV * SEG), jax.random.fold_in(arg_keys[13], 1), 0, (SUB_DEV * SEG) - 1).astype(jnp.int32)
    junc_cell = with_ends(jax.random.randint(arg_keys[14], (JUNCTIONS,), 0, BX * BY), jax.random.fold_in(arg_keys[14], 1), 0, (BX * BY) - 1).astype(jnp.int32)
    junc_owner_keys = jax.random.split(jax.random.fold_in(arg_keys[15], 1), JUNCTIONS // JUNC_DEV)
    junc_owner_turns = jax.random.permutation(jax.random.fold_in(arg_keys[15], 3), JUNCTIONS // JUNC_DEV)
    junc_owner = jax.vmap(lambda own, number: deal_out(jax.random.fold_in(arg_keys[15], 2), own, number, JUNC_DEV, DEVICES, 1, CAP, 2))(junc_owner_keys, junc_owner_turns).reshape((JUNCTIONS, 1))
    junc_gain = jnp.clip(jnp.exp(math.log(0.3) - 1.7917595 * jax.random.uniform(arg_keys[16], (JUNCTIONS,), jnp.float32) ** block_levels(arg_keys[16], (JUNCTIONS,), ((0, 16),), -0.2, 0.2)), 0.05, 0.3)
    return {"voltage": voltage, "gates": gates, "couple_x": couple_x, "couple_y": couple_y, "gate_half": gate_half, "gate_slope": gate_slope, "gate_rate": gate_rate, "conductance": conductance, "reversal": reversal, "purk_volt": purk_volt, "purk_recovery": purk_recovery, "purk_couple": purk_couple, "parent": parent, "junc_purk": junc_purk, "junc_cell": junc_cell, "junc_owner": junc_owner, "junc_gain": junc_gain}


def solve_columns(lower_band, middle_band, upper_band, source_term):
    zero_row = jnp.zeros(source_term.shape[1], source_term.dtype)

    def forward(carried, row_terms):
        factor_before, offset_before = carried
        lower_now, middle_now, upper_now, source_now = row_terms
        pivot_value = middle_now - lower_now * factor_before
        factor_now = upper_now / pivot_value
        offset_now = (source_now - lower_now * offset_before) / pivot_value
        return (factor_now, offset_now), (factor_now, offset_now)

    _, (factors, offsets) = lax.scan(forward, (zero_row, zero_row), (lower_band, middle_band, upper_band, source_term))

    def backward(next_value, row_terms):
        factor_now, offset_now = row_terms
        value_now = offset_now - factor_now * next_value
        return value_now, value_now

    _, solved = lax.scan(backward, zero_row, (factors, offsets), reverse=True)
    return solved


def reference(voltage, gates, couple_x, couple_y, gate_half, gate_slope, gate_rate, conductance, reversal,
              purk_volt, purk_recovery, purk_couple, parent, junc_purk, junc_cell, junc_owner, junc_gain):
    total_rows, total_cols = voltage.shape
    total_subs, seg_len = purk_volt.shape
    owner_device = junc_owner[:, 0]
    source = jnp.arange(junc_purk.shape[0], dtype=jnp.int32) // JUNC_DEV
    cell_row = (owner_device // N_XY) * BX + junc_cell // BY
    cell_col = (owner_device % N_XY) * BY + junc_cell % BY
    cell_index = (cell_row * total_cols + cell_col).astype(jnp.int32)
    node_index = (source * (SUB_DEV * SEG) + junc_purk).astype(jnp.int32)

    row_ids = jnp.arange(total_rows, dtype=jnp.int32)[:, None]
    lower_band = jnp.where(row_ids > 0, -couple_x, 0.0)
    upper_band = jnp.where(row_ids < total_rows - 1, -couple_x, 0.0)
    middle_band = 1.0 + jnp.where(row_ids > 0, couple_x, 0.0) + jnp.where(row_ids < total_rows - 1, couple_x, 0.0)

    subtree_ids = jnp.arange(total_subs, dtype=jnp.int32)
    has_parent = parent >= 0
    parent_hot = (subtree_ids[None, :] == parent[:, None]).astype(jnp.float32)
    child_hot = (parent[None, :] == subtree_ids[:, None]).astype(jnp.float32)
    child_count = jnp.sum(child_hot, axis=1)

    decay_factor = jnp.exp(-gate_rate)[:, None, None]
    gate_mid = gate_half[:, None, None]
    gate_steep = gate_slope[:, None, None]
    weight = conductance[:, None, None]
    driven_weight = (conductance * reversal)[:, None, None]

    def advance(step_index, current_state):
        membrane, gating, purkinje, recovery = current_state
        current = junc_gain * (purkinje.reshape(-1)[node_index] - membrane.reshape(-1)[cell_index])
        steady = jax.nn.sigmoid((membrane[None] - gate_mid) * gate_steep)
        gating = steady + (gating - steady) * decay_factor
        ionic_flux = membrane * jnp.sum(weight * gating, axis=0) - jnp.sum(driven_weight * gating, axis=0)
        inject = jax.ops.segment_sum(current, cell_index, num_segments=total_rows * total_cols).reshape(total_rows, total_cols)
        padded = jnp.concatenate([membrane[:, :1], membrane, membrane[:, -1:]], axis=1)
        source_term = membrane - ionic_flux + inject + couple_y * (padded[:, :-2] + padded[:, 2:] - 2.0 * membrane)
        membrane_next = solve_columns(lower_band, middle_band, upper_band, source_term)

        parent_last = jnp.dot(parent_hot, purkinje[:, -1], precision=lax.Precision.HIGHEST)
        child_first = jnp.dot(child_hot, purkinje[:, 0], precision=lax.Precision.HIGHEST)
        head_value = jnp.where(has_parent, parent_last, purkinje[:, 0])
        left_side = jnp.concatenate([head_value[:, None], purkinje[:, :-1]], axis=1)
        right_side = jnp.concatenate([purkinje[:, 1:], purkinje[:, -1:]], axis=1)
        spread = left_side + right_side - 2.0 * purkinje
        spread = spread.at[:, -1].add(child_first - child_count * purkinje[:, -1])
        junction_draw = jax.ops.segment_sum(current, node_index, num_segments=total_subs * seg_len).reshape(total_subs, seg_len)
        purkinje_next = (purkinje + purk_couple * spread + 0.2 * purkinje * (purkinje - 0.15) * (1.0 - purkinje)
                         - 0.1 * recovery - junction_draw)
        recovery_next = recovery + 0.05 * (purkinje - 0.5 * recovery)
        return (membrane_next, gating, purkinje_next, recovery_next)

    membrane, gating, purkinje, recovery = lax.fori_loop(0, STEPS, advance, (voltage, gates, purk_volt, purk_recovery))
    return membrane, gating, purkinje, recovery
```

```python
import jax
import jax.numpy as jnp
from jax import lax
from jax.experimental import pallas as pl
from jax.experimental.pallas import tpu as pltpu
from jax.sharding import PartitionSpec as P

STEPS = 16
HALO = 16
CAP = 4
OWN = 8
BRICK = 8
LANE = 128
WING = 32
F32 = jnp.float32
BF16 = jnp.bfloat16


def split3(value):
    high = value.astype(BF16)
    rest = value - high.astype(F32)
    mid = rest.astype(BF16)
    low = (rest - mid.astype(F32)).astype(BF16)
    return high, mid, low


def cut3(value):
    high = lax.reduce_precision(value, 8, 7)
    rest = value - high
    mid = lax.reduce_precision(rest, 8, 7)
    return high.astype(BF16), mid.astype(BF16), (rest - mid).astype(BF16)


def hot_dot(hot, value):
    parts = jnp.concatenate(cut3(value), axis=-1)
    got = jnp.dot(hot, parts, preferred_element_type=F32)
    n = value.shape[-1]
    return got[..., :n] + got[..., n : 2 * n] + got[..., 2 * n :]


def green_kernel(c_ref, u_ref, w_ref, i_ref):
    rows = c_ref.shape[0]
    inv = 1.0 / c_ref[...]
    i_ref[...] = inv
    u = jnp.ones_like(c_ref[0:1, :])
    d = jnp.zeros_like(u)
    u_ref[0:1, :] = u
    for i in range(rows - 1):
        d = d + u * i_ref[i : i + 1, :]
        u = u + d
        u_ref[i + 1 : i + 2, :] = u
    w = jnp.ones_like(u)
    e = w * i_ref[rows - 1 : rows, :]
    wronskian = d * (w + e) + (u - d) * e
    scale = 1.0 / wronskian
    w_ref[rows - 1 : rows, :] = w * scale
    w = w + e
    w_ref[rows - 2 : rows - 1, :] = w * scale
    for i in range(rows - 2, 0, -1):
        e = e + w * i_ref[i : i + 1, :]
        w = w + e
        w_ref[i - 1 : i, :] = w * scale


def green(c):
    out = jax.ShapeDtypeStruct(c.shape, F32)
    return pl.pallas_call(green_kernel, out_shape=(out, out, out), name="green")(c)


def lanes():
    return lax.broadcasted_iota(jnp.int32, (BRICK, LANE), 1)


def sublanes():
    return lax.broadcasted_iota(jnp.int32, (BRICK, LANE), 0)


def wide3(value):
    return jnp.concatenate(split3(value), axis=1)


def fold3(value):
    return value[:, :LANE] + value[:, LANE : 2 * LANE] + value[:, 2 * LANE :]


def neighbours(m, at_left, at_right):
    lane = lanes()
    c = lane % WING
    left, right = [], []
    for b in range(OWN):
        h, base = OWN + b // 4, (b % 4) * WING
        edge = pltpu.roll(m[h], (LANE - (base + HALO - 1)) % LANE, 1)
        edge = jnp.where(at_left, m[b], edge)
        left.append(jnp.where(lane == 0, edge, pltpu.roll(m[b], 1, 1)))
        edge = pltpu.roll(m[h], (LANE - 1 - (base + HALO)) % LANE, 1)
        edge = jnp.where(at_right, m[b], edge)
        right.append(jnp.where(lane == LANE - 1, edge, pltpu.roll(m[b], LANE - 1, 1)))
    for h in range(2):
        v = m[OWN + h]
        lf = jnp.where(c == 0, v, pltpu.roll(v, 1, 1))
        rt = jnp.where(c == WING - 1, v, pltpu.roll(v, LANE - 1, 1))
        for k in range(4):
            own, base = m[h * 4 + k], k * WING
            lf = jnp.where(lane == base + HALO, pltpu.roll(own, (base + HALO + 1) % LANE, 1), lf)
            rt = jnp.where(lane == base + HALO - 1, pltpu.roll(own, (base + HALO - 1) % LANE, 1), rt)
        left.append(lf)
        right.append(rt)
    return left, right


def gate_step(m, par_ref, flag_ref, cy_ref, gate_in, gate_out):
    zero = jnp.zeros((BRICK, LANE), F32)
    nb = OWN + 2

    def body(k, carried):
        total, push = carried
        half, slope, decay = par_ref[0, k], par_ref[1, k], par_ref[2, k]
        weight, driven = par_ref[3, k], par_ref[4, k]
        total_next, push_next = [], []
        for b in range(nb):
            steady = 0.5 + 0.5 * jnp.tanh((m[b] - half) * slope)
            gate = steady + (gate_in[b, k] - steady) * decay
            gate_out[b, k] = gate
            total_next.append(total[b] + weight * gate)
            push_next.append(push[b] + driven * gate)
        return tuple(total_next), tuple(push_next)

    start = (tuple([zero] * nb), tuple([zero] * nb))
    total, push = lax.fori_loop(0, gate_in.shape[1], body, start, unroll=2)
    left, right = neighbours(m, flag_ref[0] > 0, flag_ref[1] > 0)
    return [
        m[b] - (m[b] * total[b] - push[b]) + cy_ref[b] * (left[b] + right[b] - 2.0 * m[b])
        for b in range(nb)
    ]


def solve(source, u_ref, w_ref, ic_ref):
    row, lane = sublanes(), lanes()
    nb = OWN + 2
    before, after, total_b, total_a = [], [], [], []
    for b in range(nb):
        s = source[b] * ic_ref[b]
        p = u_ref[b] * s
        q = w_ref[b] * s
        for step in (1, 2, 4):
            p = p + jnp.where(row >= step, pltpu.roll(p, step, 0), 0.0)
            q = q + jnp.where(row < BRICK - step, pltpu.roll(q, BRICK - step, 0), 0.0)
        total_b.append(jnp.broadcast_to(p[BRICK - 1 : BRICK, :], p.shape))
        total_a.append(jnp.broadcast_to(q[0:1, :], q.shape))
        before.append(p)
        after.append(jnp.where(row < BRICK - 1, pltpu.roll(q, BRICK - 1, 0), 0.0))
    run = None
    for b in range(OWN):
        if run is not None:
            before[b] = before[b] + run
        run = total_b[b] if run is None else run + total_b[b]
    run = None
    for b in range(OWN - 1, -1, -1):
        if run is not None:
            after[b] = after[b] + run
        run = total_a[b] if run is None else run + total_a[b]

    def scan4(t, up):
        shift = (lambda v, n: pltpu.roll(v, n, 1)) if up else (lambda v, n: pltpu.roll(v, LANE - n, 1))
        ok = (lambda n: lane >= n) if up else (lambda n: lane < LANE - n)
        one = t + jnp.where(ok(WING), shift(t, WING), 0.0)
        two = one + jnp.where(ok(2 * WING), shift(one, 2 * WING), 0.0)
        return jnp.where(ok(WING), shift(two, WING), 0.0)

    def all4(t):
        two = t + pltpu.roll(t, WING, 1)
        return two + pltpu.roll(two, 2 * WING, 1)

    before[OWN] = before[OWN] + scan4(total_b[OWN], True)
    before[OWN + 1] = before[OWN + 1] + scan4(total_b[OWN + 1], True) + all4(total_b[OWN])
    after[OWN + 1] = after[OWN + 1] + scan4(total_a[OWN + 1], False)
    after[OWN] = after[OWN] + scan4(total_a[OWN], False) + all4(total_a[OWN + 1])
    return [w_ref[b] * before[b] + u_ref[b] * after[b] for b in range(nb)]


def sample(m, count, t):
    big = wide3(jnp.concatenate(m[:OWN], axis=0))

    def body(b, msg):
        at = pl.ds(pl.multiple_of(b * LANE, LANE), LANE)
        picked = fold3(jnp.dot(t["row_t"][at, :], big, preferred_element_type=F32))
        picked = jnp.where(t["gain_own"][at, :] > 0.0, picked, 0.0)
        value = jnp.sum(picked, axis=1, keepdims=True)
        value = wide3(value * t["slot_lane"][at, :])
        return msg + fold3(jnp.dot(t["slot_row"][b], value, preferred_element_type=F32))

    return lax.fori_loop(0, count, body, jnp.zeros((16, LANE), F32))


def send(early, late, msg_out):
    both = jnp.concatenate([early[:4], late[:4]], axis=0)
    for i in range(msg_out.shape[0]):
        msg_out[i] = both


def inject(m, count, purk_parts, t):
    nr = OWN * BRICK

    def body(b, carried):
        own, halo = carried
        at = pl.ds(pl.multiple_of(b * LANE, LANE), LANE)
        got = fold3(jnp.dot(t["sub"][at, :], purk_parts[...], preferred_element_type=F32))
        volts = jnp.sum(got * t["q"][at, :], axis=1, keepdims=True)
        row = t["row"][b]
        own = own + fold3(
            jnp.dot(row[:nr], wide3(volts * t["gain_own"][at, :]), preferred_element_type=F32)
        )
        halo = halo + fold3(
            jnp.dot(row[nr:], wide3(volts * t["gain_halo"][at, :]), preferred_element_type=F32)
        )
        return own, halo

    start = (jnp.zeros((nr, LANE), F32), jnp.zeros((2 * BRICK, LANE), F32))
    own, halo = lax.fori_loop(0, count, body, start)
    parts = [own[b * BRICK : (b + 1) * BRICK] for b in range(OWN)]
    parts += [halo[:BRICK], halo[BRICK:]]
    return [parts[b] - t["cell_gain"][b] * m[b] for b in range(OWN + 2)]


def to_nodes(tile, hot_sub, hot_q, out_ref):
    subs = hot_sub.shape[2]
    for s in range(hot_q.shape[0]):
        rows = []
        for time in range(2):
            high, low = [], []
            for xh in range(4):
                r = tile[xh][s % 4][time * 4 + s // 4 : time * 4 + s // 4 + 1, :]
                hot = hot_sub[s, xh]
                up = r.astype(BF16).astype(F32)
                high.append(hot * jnp.broadcast_to(up, (subs, LANE)).astype(BF16))
                low.append(hot * jnp.broadcast_to(r - up, (subs, LANE)).astype(BF16))
            rows += [jnp.concatenate(high, axis=1), jnp.concatenate(low, axis=1)]
        got = jnp.dot(jnp.concatenate(rows, axis=0), hot_q[s], preferred_element_type=F32)
        out_ref[0, s * subs : (s + 1) * subs, :] = got[:subs] + got[subs : 2 * subs]
        out_ref[1, s * subs : (s + 1) * subs, :] = got[2 * subs : 3 * subs] + got[3 * subs :]


def node_gain_kernel(gain_ref, hot_sub, hot_q, out_ref, both):
    tile = [[gain_ref[xh, a] for a in range(4)] for xh in range(4)]
    to_nodes(tile, hot_sub, hot_q, both)
    out_ref[...] = both[0]


def arrange(recv_ref, gain_ref):
    group = lanes() // WING
    summed = []
    for x in range(recv_ref.shape[1]):
        v = recv_ref[0, x]
        for g in range(1, recv_ref.shape[0]):
            v = v + recv_ref[g, x]
        summed.append(v)
    tile = []
    for xh in range(4):
        row = []
        for a in range(4):
            v = None
            for b in range(4):
                piece = summed[xh * 4 + b]
                if a != b:
                    piece = pltpu.roll(piece, ((b - a) * WING) % LANE, 1)
                v = piece if v is None else jnp.where(group == b, piece, v)
            row.append(v * gain_ref[xh, a])
        tile.append(row)
    return tile


def purk_step(purk, rec, drawn, t):
    nodes = purk.shape[0]
    lane = lax.broadcasted_iota(jnp.int32, purk.shape, 1)
    high, mid, low = (v.astype(F32) for v in split3(purk))
    last = LANE - 1
    ends = jnp.where(lane == last, high, 0.0) + jnp.where(lane == 0, high, 0.0)
    ends = jnp.where(lane == last - 1, pltpu.roll(mid, last, 1), ends)
    ends = jnp.where(lane == last - 2, pltpu.roll(low, last - 1, 1), ends)
    ends = jnp.where(lane == 1, pltpu.roll(mid, 1, 1), ends)
    ends = jnp.where(lane == 2, pltpu.roll(low, 2, 1), ends)
    kin = jnp.dot(t["family"][...], ends.astype(BF16), preferred_element_type=F32)
    up, down = kin[:nodes], kin[nodes:]
    up = up + pltpu.roll(up, 1, 1) + pltpu.roll(up, 2, 1)
    down = down + pltpu.roll(down, last, 1) + pltpu.roll(down, last - 1, 1)
    left = pltpu.roll(jnp.where(lane == last, up, purk), 1, 1)
    left = jnp.where(t["self_head"][...] > 0.0, purk, left)
    right = jnp.where(lane == last, purk, pltpu.roll(purk, last, 1))
    spread = left + right - 2.0 * purk
    extra = pltpu.roll(down, last, 1) - t["children"][...] * purk
    spread = spread + jnp.where(lane == last, extra, 0.0)
    purk_next = (
        purk
        + t["couple"][...] * spread
        + 0.2 * purk * (purk - 0.15) * (1.0 - purk)
        - 0.1 * rec
        - (t["node_gain"][...] * purk - drawn)
    )
    return purk_next, rec + 0.05 * (purk - 0.5 * rec)


TABLES = (
    "gain_halo", "gain_own", "q", "slot_lane", "row_t", "sub", "row", "slot_row", "cell_gain",
)
TREE = ("family", "self_head", "children", "couple", "node_gain")


def gate_kernel(par_ref, flag_ref, mem_ref, cy_ref, gate_ref, gate_out, source_out):
    m = [mem_ref[b] for b in range(OWN + 2)]
    source = gate_step(m, par_ref, flag_ref, cy_ref, gate_ref, gate_out)
    for b in range(OWN + 2):
        source_out[b] = source[b]


def first_kernel(flag_ref, mem_ref, source_ref, purk_ref, u_ref, w_ref, ic_ref, *rest):
    t = dict(zip(TABLES, rest[: len(TABLES)]))
    mem_out, msg_out, parts = rest[len(TABLES) :]
    nb = OWN + 2
    count = flag_ref[2]
    m = [mem_ref[b] for b in range(nb)]
    early = sample(m, count, t)
    parts[...] = wide3(purk_ref[...])
    add = inject(m, count, parts, t)
    m = solve([source_ref[b] + add[b] for b in range(nb)], u_ref, w_ref, ic_ref)
    for b in range(nb):
        mem_out[b] = m[b]
    send(early, sample(m, count, t), msg_out)


def step_kernel(final, *refs):
    flag_ref, recv_ref, gain_ref, hot_sub, hot_q = refs[:5]
    mem_ref, source_ref, purk_ref, rec_ref, u_ref, w_ref, ic_ref = refs[5:12]
    at = 12 + len(TABLES)
    t = dict(zip(TABLES, refs[12:at]))
    t.update(zip(TREE, refs[at : at + len(TREE)]))
    rest = refs[at + len(TREE) :]
    if final:
        mem_out, purk_out, rec_out, parts, drawn = rest
    else:
        par_ref, cy_ref, gate_ref, mem_out, purk_out, rec_out, gate_out, msg_out, parts, drawn = rest
    nb = OWN + 2
    count = flag_ref[2]
    to_nodes(arrange(recv_ref, gain_ref), hot_sub, hot_q, drawn)
    m = [mem_ref[b] for b in range(nb)]
    purk, rec = purk_step(purk_ref[...], rec_ref[...], drawn[0], t)
    purk_out[...] = purk
    rec_out[...] = rec
    parts[...] = wide3(purk)
    add = inject(m, count, parts, t)
    m = solve([source_ref[b] + add[b] for b in range(nb)], u_ref, w_ref, ic_ref)
    purk, rec = purk_step(purk_out[...], rec_out[...], drawn[1], t)
    purk_out[...] = purk
    rec_out[...] = rec
    if not final:
        early = sample(m, count, t)
        parts[...] = wide3(purk)
        source = gate_step(m, par_ref, flag_ref, cy_ref, gate_ref, gate_out)
        add = inject(m, count, parts, t)
        m = solve([source[b] + add[b] for b in range(nb)], u_ref, w_ref, ic_ref)
        send(early, sample(m, count, t), msg_out)
    for b in range(nb):
        mem_out[b] = m[b]


VMEM = pl.BlockSpec()
SMEM = pl.BlockSpec(memory_space=pltpu.SMEM)


def shape(*dims):
    return jax.ShapeDtypeStruct(dims, F32)


def on_device(
    voltage,
    gates,
    couple_x,
    couple_y,
    gate_half,
    gate_slope,
    gate_rate,
    conductance,
    reversal,
    purk_volt,
    purk_recovery,
    purk_couple,
    parent,
    junc_purk,
    junc_cell,
    junc_owner,
    junc_gain,
):
    rows, cols = voltage.shape
    subs, seg = purk_volt.shape
    gz = lax.axis_size("gz")
    xy = lax.axis_size("xy")
    g = lax.axis_index("gz")
    x = lax.axis_index("xy")
    nvar = gates.shape[0]
    chunk = cols // gz
    wide = chunk + 2 * HALO
    total_rows = rows * gz
    nodes = parent.shape[0]
    nj = junc_gain.shape[0]
    slots = gz * CAP
    per_s = xy * slots

    owner = junc_owner[:, 0]
    same = owner[:, None] == owner[None, :]
    before = jnp.arange(nj)[:, None] > jnp.arange(nj)[None, :]
    rank = jnp.sum(jnp.logical_and(same, before).astype(jnp.int32), axis=1)
    slot = (owner % xy) * slots + (owner // xy) * CAP + rank
    hot = jnp.arange(per_s, dtype=jnp.int32)[:, None] == slot[None, :]

    def place(field):
        return jnp.sum(jnp.where(hot, field[None, :], 0.0), axis=1)

    table = jnp.stack(
        [place(junc_gain), place(junc_purk.astype(F32)), place(junc_cell.astype(F32))]
    )

    mine = jnp.concatenate(
        [purk_volt.reshape(-1, seg), purk_recovery.reshape(-1, seg), purk_couple.reshape(-1, seg), table.reshape(-1, seg)]
    )
    allp = lax.all_to_all(
        jnp.broadcast_to(mine[None], (xy,) + mine.shape), "xy", 0, 0, tiled=True
    )
    purk0 = allp[:, :subs].reshape(nodes, seg)
    rec0 = allp[:, subs : 2 * subs].reshape(nodes, seg)
    pcoup = allp[:, 2 * subs : 3 * subs].reshape(nodes, seg)
    tabs = allp[:, 3 * subs :].reshape(xy, 3, xy, slots)

    slab = jnp.concatenate([gates, voltage[None], couple_x[None], couple_y[None]])
    nf = nvar + 3
    left = lax.ppermute(slab[:, :, cols - HALO :], "xy", [(i, i + 1) for i in range(xy - 1)])
    right = lax.ppermute(slab[:, :, :HALO], "xy", [(i + 1, i) for i in range(xy - 1)])
    own_part = jnp.transpose(slab.reshape(nf, rows, gz, chunk), (2, 0, 1, 3))
    lefts = jnp.concatenate([left[None], own_part[:-1, :, :, chunk - HALO :]])
    rights = jnp.concatenate([own_part[1:, :, :, :HALO], right[None]])
    halo_part = jnp.concatenate([lefts, rights], axis=-1)
    packed = jnp.concatenate(
        [own_part.reshape(gz, -1, chunk), halo_part.reshape(gz, -1, chunk)], axis=1
    )
    packed = lax.all_to_all(packed, "gz", 0, 0, tiled=True)
    own = packed[:, : nf * rows].reshape(gz, nf, rows, chunk)
    halo = packed[:, nf * rows :].reshape(gz, nf, rows, 2 * HALO)
    halo = jnp.transpose(halo.reshape(2, 4, nf, rows, WING), (0, 2, 3, 1, 4))
    halo = halo.reshape(2, nf, rows, LANE)
    full = jnp.concatenate([own, halo])
    gate = full[:, :nvar]
    mem = full[:, nvar]
    cx = jnp.maximum(full[:, nvar + 1], 1.0)
    cy = full[:, nvar + 2]
    nb = gz + 2

    def unpack(v):
        wings = jnp.transpose(v[gz:].reshape(2, rows, 4, WING), (0, 2, 1, 3))
        return jnp.concatenate(
            [v[:gz].reshape(total_rows, chunk), wings.reshape(total_rows, WING)], axis=1
        )

    def pack(v):
        wings = jnp.transpose(v[:, chunk:].reshape(2, 4, rows, WING), (0, 2, 1, 3))
        return jnp.concatenate(
            [v[:, :chunk].reshape(gz, rows, chunk), wings.reshape(2, rows, LANE)]
        )

    gu, gw, ginv = (pack(v) for v in green(unpack(cx)))

    def side(which, shift):
        tab = lax.dynamic_index_in_dim(tabs, which, 2, keepdims=False)
        cell = tab[:, 2].reshape(xy, gz, CAP).astype(jnp.int32)
        purk = tab[:, 1].reshape(xy, gz, CAP).astype(jnp.int32)
        brick = jnp.arange(gz, dtype=jnp.int32)[None, :, None]
        row = brick * rows + cell // cols
        place_at = cell % cols + shift * cols - g * chunk + HALO
        sub = jnp.arange(xy, dtype=jnp.int32)[:, None, None] * subs + purk // seg
        return tuple(
            v.reshape(-1) for v in (tab[:, 0].reshape(xy, gz, CAP), row, place_at, sub, purk % seg)
        )

    gain_a, row_a, col_a, sub_a, q_a = side(x, 0)
    go_left = g == 0
    shift = jnp.where(go_left, -1, 1)
    other = x + shift
    near = jnp.logical_and(
        jnp.logical_or(go_left, g == gz - 1), jnp.logical_and(other >= 0, other < xy)
    )
    gain_b, row_b, col_b, sub_b, q_b = side(jnp.clip(other, 0, xy - 1), shift)
    gain_b = jnp.where(near, gain_b, 0.0)
    gain = jnp.concatenate([gain_a, gain_b])
    place_at = jnp.concatenate([col_a, col_b])
    number = jnp.arange(2 * per_s, dtype=jnp.int32)
    inside = jnp.logical_and(place_at >= HALO, place_at < HALO + chunk)
    sent = jnp.where(jnp.logical_and(inside, number < per_s), number, -1)
    fields = jnp.stack(
        [gain]
        + [
            v.astype(F32)
            for v in (
                jnp.concatenate([row_a, row_b]),
                place_at,
                jnp.concatenate([sub_a, sub_b]),
                jnp.concatenate([q_a, q_b]),
                sent,
            )
        ]
    )
    relevant = jnp.logical_and(
        gain > 0.0, jnp.logical_and(place_at >= 0, place_at < chunk + 2 * HALO)
    )
    until = jnp.cumsum(relevant.astype(jnp.int32))
    count = (until[-1] + LANE - 1) // LANE
    target = jnp.where(relevant, until - 1, -1)
    hot = (target[:, None] == number[None, :]).astype(BF16)
    got = jnp.dot(jnp.concatenate(cut3(fields)), hot, preferred_element_type=F32)
    nfield = fields.shape[0]
    packed_rows = got[:nfield] + got[nfield : 2 * nfield] + got[2 * nfield :]
    packed_cols = packed_rows.T
    alive = number < until[-1]

    def as_int(v):
        return v.astype(jnp.int32)

    gain_c = packed_cols[:, 0:1]
    row_c, col_c, sub_c, q_c, sent_c = (
        jnp.where(alive[:, None], as_int(packed_cols[:, i : i + 1]), -1) for i in range(1, 6)
    )
    row_r, sent_r = (jnp.where(alive, as_int(packed_rows[i]), -1) for i in (1, 5))
    lane = jnp.arange(LANE, dtype=jnp.int32)[None, :]
    wing_at = jnp.where(col_c < HALO, col_c, col_c - chunk)
    wing = jnp.logical_or(
        jnp.logical_and(col_c >= 0, col_c < HALO), col_c >= HALO + chunk
    )
    wing_at = jnp.where(wing, (row_c // rows % 4) * WING + wing_at, -1)
    t = {}
    t["gain_halo"] = jnp.where(wing_at == lane, gain_c, 0.0)
    t["gain_own"] = jnp.where(col_c - HALO == lane, gain_c, 0.0)
    t["q"] = (q_c == lane).astype(F32)
    t["slot_lane"] = (jnp.where(sent_c >= 0, sent_c % LANE, -1) == lane).astype(F32)
    t["row_t"] = (row_c == jnp.arange(total_rows)[None, :]).astype(BF16)
    t["sub"] = (sub_c == jnp.arange(nodes)[None, :]).astype(BF16)
    blocks = 2 * per_s // LANE
    row_b = row_r.reshape(blocks, 1, LANE)
    halo_row = (row_b // rows // 4) * rows + row_b % rows
    t["row"] = jnp.concatenate(
        [
            row_b == jnp.arange(total_rows)[None, :, None],
            jnp.logical_and(row_b >= 0, halo_row == jnp.arange(2 * rows)[None, :, None]),
        ],
        axis=1,
    ).astype(BF16)
    sent_b = sent_r.reshape(blocks, 1, LANE)
    t["slot_row"] = (
        jnp.where(sent_b >= 0, sent_b // LANE, -1) == jnp.arange(16)[None, :, None]
    ).astype(BF16)
    flat_row = jnp.transpose(t["row"], (1, 0, 2)).reshape(total_rows + 2 * rows, -1)
    t["cell_gain"] = jnp.concatenate(
        [
            hot_dot(flat_row[:total_rows], t["gain_own"]).reshape(gz, rows, LANE),
            hot_dot(flat_row[total_rows:], t["gain_halo"]).reshape(2, rows, LANE),
        ]
    )

    gain_p = tabs[:, 0].reshape(4, 4, 4, LANE)
    gain_t = jnp.transpose(gain_p, (2, 1, 0, 3))
    gain_t = jnp.concatenate([gain_t, gain_t], axis=2)
    node_p = tabs[:, 1].reshape(xy, per_s).astype(jnp.int32)
    sub_p = (node_p // seg).reshape(xy, 4, 1, LANE)
    hot_sub_p = (sub_p == jnp.arange(subs, dtype=jnp.int32)[None, None, :, None]).astype(BF16)
    hot_q_p = ((node_p % seg)[:, :, None] == jnp.arange(seg)[None, None, :]).astype(BF16)
    t["node_gain"] = pl.pallas_call(
        node_gain_kernel,
        out_shape=shape(nodes, seg),
        scratch_shapes=[pltpu.VMEM((2, nodes, seg), F32)],
        name="node_gain",
    )(gain_t, hot_sub_p, hot_q_p)
    all_ids = jnp.arange(nodes, dtype=jnp.int32)
    parent_hot = (all_ids[None, :] == parent[:, None]).astype(BF16)
    child_hot = (parent[None, :] == all_ids[:, None]).astype(BF16)
    t["family"] = jnp.concatenate([parent_hot, child_hot])
    t["children"] = jnp.broadcast_to(
        jnp.sum(child_hot.astype(F32), axis=1, keepdims=True), (nodes, seg)
    )
    t["self_head"] = jnp.logical_and((parent < 0)[:, None], lane == 0).astype(F32)
    t["couple"] = pcoup

    par = jnp.stack(
        [gate_half, 0.5 * gate_slope, jnp.exp(-gate_rate), conductance, conductance * reversal]
    )
    flags = jnp.stack(
        [
            jnp.logical_and(x == 0, g == 0).astype(jnp.int32),
            jnp.logical_and(x == xy - 1, g == gz - 1).astype(jnp.int32),
            count.astype(jnp.int32),
        ]
    )
    t, gain_t, hot_sub_p, hot_q_p = lax.optimization_barrier((t, gain_t, hot_sub_p, hot_q_p))
    tables = [t[name] for name in TABLES]
    tree = [t[name] for name in TREE]
    slab_shape = shape(nb, rows, LANE)
    node_shape = shape(nodes, seg)
    gate_shape = shape(nb, nvar, rows, LANE)
    msg_shape = shape(gz * xy, 8, LANE)
    parts = pltpu.VMEM((nodes, 3 * LANE), BF16)
    drawn = pltpu.VMEM((2, nodes, seg), F32)
    limit = pltpu.CompilerParams(vmem_limit_bytes=24 << 20)
    solver = [gu, gw, ginv]

    def gate_call(mem, gate):
        return pl.pallas_call(
            gate_kernel,
            out_shape=(gate_shape, slab_shape),
            in_specs=[SMEM, SMEM, VMEM, VMEM, VMEM],
            out_specs=(VMEM, VMEM),
            input_output_aliases={4: 0},
            compiler_params=limit,
            cost_estimate=pl.CostEstimate(flops=8_000_000, transcendentals=900_000, bytes_accessed=3_400_000),
            name="gate",
        )(par, flags, mem, cy, gate)

    def exchange(msg):
        got = lax.all_to_all(msg, ("gz", "xy"), 0, 0, tiled=True)
        return got.reshape(gz, xy, 8, LANE)

    def step_call(final, recv, mem, source, purk, rec, gate):
        args = [flags, recv, gain_t, hot_sub_p, hot_q_p, mem, source, purk, rec]
        args += solver + tables + tree
        outs = [slab_shape, node_shape, node_shape]
        alias = {}
        if not final:
            args += [par, cy, gate]
            alias = {5: 0, 7: 1, 8: 2, len(args) - 1: 3}
            outs += [gate_shape, msg_shape]
        specs = [VMEM] * len(args)
        specs[0] = SMEM
        if not final:
            specs[-3] = SMEM
        return pl.pallas_call(
            lambda *refs: step_kernel(final, *refs),
            out_shape=tuple(outs),
            in_specs=specs,
            out_specs=tuple([VMEM] * len(outs)),
            scratch_shapes=[parts, drawn],
            input_output_aliases=alias,
            compiler_params=limit,
            name="last" if final else "step",
        )(*args)

    gate, source = gate_call(mem, gate)
    mem, msg = pl.pallas_call(
        first_kernel,
        out_shape=(slab_shape, msg_shape),
        in_specs=[SMEM] + [VMEM] * (6 + len(TABLES)),
        out_specs=(VMEM, VMEM),
        scratch_shapes=[parts],
        compiler_params=limit,
        name="first",
    )(flags, mem, source, purk0, *solver, *tables)

    def two(k, state):
        mem, gate, purk, rec, msg = state
        recv = exchange(msg)
        gate, source = gate_call(mem, gate)
        mem, purk, rec, gate, msg = step_call(False, recv, mem, source, purk, rec, gate)
        return mem, gate, purk, rec, msg

    mem, gate, purk, rec, msg = lax.fori_loop(
        0, STEPS // 2 - 1, two, (mem, gate, purk0, rec0, msg)
    )
    recv = exchange(msg)
    gate, source = gate_call(mem, gate)
    mem, purk, rec = step_call(True, recv, mem, source, purk, rec, gate)

    back = jnp.concatenate([gate[:gz], mem[:gz, None]], axis=1).reshape(gz, -1, chunk)
    back = lax.all_to_all(back, "gz", 0, 0, tiled=True)
    back = back.reshape(gz, nvar + 1, rows, chunk)
    back = jnp.transpose(back, (1, 2, 0, 3)).reshape(nvar + 1, rows, cols)
    purk_mine = lax.dynamic_slice_in_dim(purk, x * subs, subs, axis=0)
    rec_mine = lax.dynamic_slice_in_dim(rec, x * subs, subs, axis=0)
    return back[nvar], back[:nvar], purk_mine, rec_mine


def solution(mesh):
    return jax.shard_map(
        on_device,
        mesh=mesh,
        in_specs=(
            P("gz", "xy"),
            P(None, "gz", "xy"),
            P("gz", "xy"),
            P("gz", "xy"),
            P(),
            P(),
            P(),
            P(),
            P(),
            P("xy", None),
            P("xy", None),
            P("xy", None),
            P(),
            P("xy"),
            P("xy"),
            P("xy", None),
            P("xy"),
        ),
        out_specs=(P("gz", "xy"), P(None, "gz", "xy"), P("xy", None), P("xy", None)),
        check_vma=False,
    )
```

```python
import jax
import jax.numpy as jnp
from jax import lax
from jax.experimental import pallas as pl
from jax.experimental.pallas import tpu as pltpu
from jax.sharding import PartitionSpec as P

STEPS = 16
HALO = 16
CAP = 4
OWN = 8
BRICK = 8
LANE = 128
WING = 32
ROWS_AT = 128
F32 = jnp.float32
BF16 = jnp.bfloat16


def split3(value):
    high = value.astype(BF16)
    rest = value - high.astype(F32)
    mid = rest.astype(BF16)
    low = (rest - mid.astype(F32)).astype(BF16)
    return high, mid, low


def cut3(value):
    high = lax.reduce_precision(value, 8, 7)
    rest = value - high
    mid = lax.reduce_precision(rest, 8, 7)
    return high.astype(BF16), mid.astype(BF16), (rest - mid).astype(BF16)


def hot_dot(hot, value):
    parts = jnp.concatenate(cut3(value), axis=-1)
    got = jnp.dot(hot, parts, preferred_element_type=F32)
    n = value.shape[-1]
    return got[..., :n] + got[..., n : 2 * n] + got[..., 2 * n :]


def pack_kernel(gate_ref, volt_ref, cx_ref, cy_ref, left_ref, right_ref, out_ref):
    lane = lanes()
    nvar = gate_ref.shape[0]
    fields = nvar + 3
    chunks = out_ref.shape[0]
    extra = (volt_ref, cx_ref, cy_ref)
    span = [slice(g * LANE, (g + 1) * LANE) for g in range(chunks)]

    def put(f4, pick, count):
        for fl in range(count):
            at = pl.ds(pl.multiple_of((f4 * 4 + fl) * BRICK, BRICK), BRICK)
            for g in range(chunks):
                out_ref[g, at, :] = pick(fl, g)
        at = pl.ds(pl.multiple_of((fields + f4) * BRICK, BRICK), BRICK)
        for g in range(chunks):
            v = jnp.zeros((BRICK, LANE), F32)
            for fl in range(count):
                base = fl * WING
                low = pltpu.roll(pick(fl, g - 1), (base + HALO) % LANE, 1)
                high = pltpu.roll(pick(fl, g + 1), (base + HALO) % LANE, 1)
                v = jnp.where(jnp.logical_and(lane >= base, lane < base + HALO), low, v)
                v = jnp.where(jnp.logical_and(lane >= base + HALO, lane < base + WING), high, v)
            out_ref[g, at, :] = v

    def body(f4, carried):
        def pick(fl, g):
            f = f4 * 4 + fl
            if g < 0:
                return left_ref[f]
            return right_ref[f] if g == chunks else gate_ref[f, :, span[g]]

        put(f4, pick, 4)
        return carried

    lax.fori_loop(0, nvar // 4, body, 0)

    def pick(fl, g):
        if g < 0:
            return left_ref[nvar + fl]
        return right_ref[nvar + fl] if g == chunks else extra[fl][:, span[g]]

    put(nvar // 4, pick, 3)


def unpack_kernel(in_ref, gate_ref, mem_ref, cy_ref, u_ref, w_ref, ic_ref, near, u_far, w_far, i_far):
    nvar = gate_ref.shape[1]
    fields = nvar + 3
    group = lanes() // WING
    total = OWN * BRICK

    def gather(piece, h, fl):
        v = None
        for lg in range(4):
            part = piece(h * 4 + lg)
            if lg != fl:
                part = pltpu.roll(part, ((lg - fl) * WING) % LANE, 1)
            v = part if v is None else jnp.where(group == lg, part, v)
        return v

    def body(f4, carried):
        at = pl.ds(pl.multiple_of((fields + f4) * BRICK, BRICK), BRICK)
        for fl in range(4):
            f = f4 * 4 + fl
            own = pl.ds(pl.multiple_of(f * BRICK, BRICK), BRICK)
            for b in range(OWN):
                gate_ref[b, f] = in_ref[b, own, :]
            for h in range(2):
                gate_ref[OWN + h, f] = gather(lambda b: in_ref[b, at, :], h, fl)
        return carried

    lax.fori_loop(0, nvar // 4, body, 0)
    tail = slice((fields + nvar // 4) * BRICK, (fields + nvar // 4 + 1) * BRICK)
    for b in range(OWN):
        mem_ref[b] = in_ref[b, nvar * BRICK : (nvar + 1) * BRICK, :]
        cy_ref[b] = in_ref[b, (nvar + 2) * BRICK : (nvar + 3) * BRICK, :]
        c = in_ref[b, (nvar + 1) * BRICK : (nvar + 2) * BRICK, :]
        inv = 1.0 / c
        ic_ref[b] = inv
        near[b * BRICK : (b + 1) * BRICK, :] = inv
        c = in_ref[b, tail, :]
        i_far[b * BRICK : (b + 1) * BRICK, :] = 1.0 / jnp.where(c > 1.0, c, 300.0)
    for h in range(2):
        mem_ref[OWN + h] = gather(lambda b: in_ref[b, tail, :], h, 0)
        cy_ref[OWN + h] = gather(lambda b: in_ref[b, tail, :], h, 2)

    def put_u(i, one, two):
        u_ref[i // BRICK, i % BRICK : i % BRICK + 1, :] = one
        u_far[i : i + 1, :] = two

    def put_w(i, one, two):
        w_ref[i // BRICK, i % BRICK : i % BRICK + 1, :] = one
        w_far[i : i + 1, :] = two

    def both(i):
        return near[i : i + 1, :], i_far[i : i + 1, :]

    u = [jnp.ones((1, LANE), F32)] * 2
    d = [jnp.zeros((1, LANE), F32)] * 2
    put_u(0, *u)
    for i in range(total - 1):
        inv = both(i)
        d = [d[n] + u[n] * inv[n] for n in range(2)]
        u = [u[n] + d[n] for n in range(2)]
        put_u(i + 1, *u)
    inv = both(total - 1)
    e = list(inv)
    scale = [1.0 / (d[n] * (1.0 + e[n]) + (u[n] - d[n]) * e[n]) for n in range(2)]
    w = [jnp.ones((1, LANE), F32)] * 2
    put_w(total - 1, *(w[n] * scale[n] for n in range(2)))
    w = [w[n] + e[n] for n in range(2)]
    put_w(total - 2, *(w[n] * scale[n] for n in range(2)))
    for i in range(total - 2, 0, -1):
        inv = both(i)
        e = [e[n] + w[n] * inv[n] for n in range(2)]
        w = [w[n] + e[n] for n in range(2)]
        put_w(i - 1, *(w[n] * scale[n] for n in range(2)))
    for far, out_ref in ((u_far, u_ref), (w_far, w_ref), (i_far, ic_ref)):
        for h in range(2):
            out_ref[OWN + h] = gather(lambda b: far[b * BRICK : (b + 1) * BRICK, :], h, 1)


def lanes():
    return lax.broadcasted_iota(jnp.int32, (BRICK, LANE), 1)


def sublanes():
    return lax.broadcasted_iota(jnp.int32, (BRICK, LANE), 0)


def wide2(value):
    high = value.astype(BF16)
    return jnp.concatenate([high, (value - high.astype(F32)).astype(BF16)], axis=1)


def fold2(value):
    return value[:, :LANE] + value[:, LANE:]


def neighbours(m, at_left, at_right):
    lane = lanes()
    c = lane % WING
    left, right = [], []
    for b in range(OWN):
        h, base = OWN + b // 4, (b % 4) * WING
        edge = pltpu.roll(m[h], (LANE - (base + HALO - 1)) % LANE, 1)
        edge = jnp.where(at_left, m[b], edge)
        left.append(jnp.where(lane == 0, edge, pltpu.roll(m[b], 1, 1)))
        edge = pltpu.roll(m[h], (LANE - 1 - (base + HALO)) % LANE, 1)
        edge = jnp.where(at_right, m[b], edge)
        right.append(jnp.where(lane == LANE - 1, edge, pltpu.roll(m[b], LANE - 1, 1)))
    for h in range(2):
        v = m[OWN + h]
        lf = jnp.where(c == 0, v, pltpu.roll(v, 1, 1))
        rt = jnp.where(c == WING - 1, v, pltpu.roll(v, LANE - 1, 1))
        for k in range(4):
            own, base = m[h * 4 + k], k * WING
            lf = jnp.where(lane == base + HALO, pltpu.roll(own, (base + HALO + 1) % LANE, 1), lf)
            rt = jnp.where(lane == base + HALO - 1, pltpu.roll(own, (base + HALO - 1) % LANE, 1), rt)
        left.append(lf)
        right.append(rt)
    return left, right


def gate_step(m, par_ref, flag_ref, cy_ref, gate_in, gate_out):
    zero = jnp.zeros((BRICK, LANE), F32)
    nb = OWN + 2

    def body(k, carried):
        total, push = carried
        slope, offset, decay = par_ref[0, k], par_ref[1, k], par_ref[2, k]
        grow, weight, driven = par_ref[3, k], par_ref[4, k], par_ref[5, k]
        total_next, push_next = [], []
        for b in range(nb):
            bend = jnp.tanh(m[b] * slope - offset)
            gate = (gate_in[b, k] * decay + grow) + grow * bend
            gate_out[b, k] = gate
            total_next.append(total[b] + weight * gate)
            push_next.append(push[b] + driven * gate)
        return tuple(total_next), tuple(push_next)

    start = (tuple([zero] * nb), tuple([zero] * nb))
    total, push = lax.fori_loop(0, gate_in.shape[1], body, start, unroll=8)
    left, right = neighbours(m, flag_ref[0] > 0, flag_ref[1] > 0)
    return [
        m[b] - (m[b] * total[b] - push[b]) + cy_ref[b] * (left[b] + right[b] - 2.0 * m[b])
        for b in range(nb)
    ]


def solve(source, u_ref, w_ref, ic_ref):
    row, lane = sublanes(), lanes()
    nb = OWN + 2
    before, after, total_b, total_a = [], [], [], []
    for b in range(nb):
        s = source[b] * ic_ref[b]
        p = u_ref[b] * s
        q = w_ref[b] * s
        for step in (1, 2, 4):
            p = p + jnp.where(row >= step, pltpu.roll(p, step, 0), 0.0)
            q = q + jnp.where(row < BRICK - step, pltpu.roll(q, BRICK - step, 0), 0.0)
        total_b.append(jnp.broadcast_to(p[BRICK - 1 : BRICK, :], p.shape))
        total_a.append(jnp.broadcast_to(q[0:1, :], q.shape))
        before.append(p)
        after.append(jnp.where(row < BRICK - 1, pltpu.roll(q, BRICK - 1, 0), 0.0))
    run = None
    for b in range(OWN):
        if run is not None:
            before[b] = before[b] + run
        run = total_b[b] if run is None else run + total_b[b]
    run = None
    for b in range(OWN - 1, -1, -1):
        if run is not None:
            after[b] = after[b] + run
        run = total_a[b] if run is None else run + total_a[b]

    def scan4(t, up):
        shift = (lambda v, n: pltpu.roll(v, n, 1)) if up else (lambda v, n: pltpu.roll(v, LANE - n, 1))
        ok = (lambda n: lane >= n) if up else (lambda n: lane < LANE - n)
        one = t + jnp.where(ok(WING), shift(t, WING), 0.0)
        two = one + jnp.where(ok(2 * WING), shift(one, 2 * WING), 0.0)
        return jnp.where(ok(WING), shift(two, WING), 0.0)

    def all4(t):
        two = t + pltpu.roll(t, WING, 1)
        return two + pltpu.roll(two, 2 * WING, 1)

    before[OWN] = before[OWN] + scan4(total_b[OWN], True)
    before[OWN + 1] = before[OWN + 1] + scan4(total_b[OWN + 1], True) + all4(total_b[OWN])
    after[OWN + 1] = after[OWN + 1] + scan4(total_a[OWN + 1], False)
    after[OWN] = after[OWN] + scan4(total_a[OWN], False) + all4(total_a[OWN + 1])
    return [w_ref[b] * before[b] + u_ref[b] * after[b] for b in range(nb)]


def over_blocks(count, blk, use, start):
    def body(b, carried):
        return use(blk["f0"].at[b], blk["s0"].at[b], blk["r0"].at[b], carried)

    return lax.fori_loop(0, count, body, start)


def block_copies(b, blk, sem):
    return [
        pltpu.make_async_copy(blk[n].at[b], blk[n + "0"].at[b], sem.at[k, b])
        for k, n in enumerate("fsr")
    ]


def start_blocks(count, blk, sem):
    def body(b, carried):
        for copy in block_copies(b, blk, sem):
            copy.start()
        return carried

    lax.fori_loop(0, count, body, 0)


def wait_blocks(count, blk, sem):
    def body(b, carried):
        for copy in block_copies(b, blk, sem):
            copy.wait()
        return carried

    lax.fori_loop(0, count, body, 0)


def sample(m, count, blk):
    rows = jnp.concatenate(m[:OWN], axis=0)
    big = wide2(jnp.concatenate([rows, jnp.zeros_like(rows)], axis=0))

    def use(f, s, r, msg):
        picked = fold2(jnp.dot(r[:LANE, :], big, preferred_element_type=F32))
        picked = jnp.where(f[1] > 0.0, picked, 0.0)
        value = jnp.sum(picked, axis=1, keepdims=True)
        value = wide2(value * f[3])
        slot_row = r[ROWS_AT + 10 * BRICK : ROWS_AT + 12 * BRICK, :]
        return msg + fold2(jnp.dot(slot_row, value, preferred_element_type=F32))

    return over_blocks(count, blk, use, jnp.zeros((2 * BRICK, LANE), F32))


def send(early, late, buf, msg_out, sem):
    both = jnp.concatenate([early[:4], late[:4]], axis=0)
    n = buf.shape[0]
    for i in range(n):
        buf[i] = both
    copies = [
        pltpu.make_async_copy(buf, msg_out.at[pl.ds(i * n, n)], sem.at[i])
        for i in range(msg_out.shape[0] // n)
    ]
    for copy in copies:
        copy.start()
    return copies


def inject(m, count, purk_parts, cell_gain, blk):
    nr = OWN * BRICK

    def use(f, s, r, carried):
        own, halo = carried
        got = fold2(jnp.dot(s[...], purk_parts[...], preferred_element_type=F32))
        volts = jnp.sum(got * f[2], axis=1, keepdims=True)
        own = own + fold2(
            jnp.dot(r[ROWS_AT : ROWS_AT + nr, :], wide2(volts * f[1]), preferred_element_type=F32)
        )
        halo = halo + fold2(
            jnp.dot(
                r[ROWS_AT + nr : ROWS_AT + nr + 2 * BRICK, :],
                wide2(volts * f[0]),
                preferred_element_type=F32,
            )
        )
        return own, halo

    start = (jnp.zeros((nr, LANE), F32), jnp.zeros((2 * BRICK, LANE), F32))
    own, halo = over_blocks(count, blk, use, start)
    parts = [own[b * BRICK : (b + 1) * BRICK] for b in range(OWN)]
    parts += [halo[:BRICK], halo[BRICK:]]
    return [parts[b] - cell_gain[b] * m[b] for b in range(OWN + 2)]


def to_nodes(tile, hot_sub, hot_q, out_ref, waits=()):
    subs = hot_sub.shape[2]
    for s in range(hot_q.shape[0]):
        if waits and s % 4 == 0:
            waits[s // 4].wait()
        rows = []
        for time in range(2):
            high, low = [], []
            for xh in range(4):
                r = tile[xh][s % 4][time * 4 + s // 4 : time * 4 + s // 4 + 1, :]
                hot = hot_sub[s, xh]
                up = r.astype(BF16).astype(F32)
                high.append(hot * jnp.broadcast_to(up, (subs, LANE)).astype(BF16))
                low.append(hot * jnp.broadcast_to(r - up, (subs, LANE)).astype(BF16))
            rows += [jnp.concatenate(high, axis=1), jnp.concatenate(low, axis=1)]
        got = jnp.dot(jnp.concatenate(rows, axis=0), hot_q[s], preferred_element_type=F32)
        out_ref[0, s * subs : (s + 1) * subs, :] = got[:subs] + got[subs : 2 * subs]
        out_ref[1, s * subs : (s + 1) * subs, :] = got[2 * subs : 3 * subs] + got[3 * subs :]


def node_gain_kernel(gain_ref, hot_sub, hot_q, out_ref, both):
    tile = [[gain_ref[xh, a] for a in range(4)] for xh in range(4)]
    to_nodes(tile, hot_sub, hot_q, both)
    out_ref[...] = both[0]


def arrange(recv_ref, gain_ref):
    group = lanes() // WING
    summed = []
    for x in range(recv_ref.shape[1]):
        v = recv_ref[0, x]
        for g in range(1, recv_ref.shape[0]):
            v = v + recv_ref[g, x]
        summed.append(v)
    tile = []
    for xh in range(4):
        row = []
        for a in range(4):
            v = None
            for b in range(4):
                piece = summed[xh * 4 + b]
                if a != b:
                    piece = pltpu.roll(piece, ((b - a) * WING) % LANE, 1)
                v = piece if v is None else jnp.where(group == b, piece, v)
            row.append(v * gain_ref[xh, a])
        tile.append(row)
    return tile


def purk_step(purk, rec, drawn, t):
    nodes = purk.shape[0]
    lane = lax.broadcasted_iota(jnp.int32, purk.shape, 1)
    high, mid, low = (v.astype(F32) for v in split3(purk))
    last = LANE - 1
    ends = jnp.where(lane == last, high, 0.0) + jnp.where(lane == 0, high, 0.0)
    ends = jnp.where(lane == last - 1, pltpu.roll(mid, last, 1), ends)
    ends = jnp.where(lane == last - 2, pltpu.roll(low, last - 1, 1), ends)
    ends = jnp.where(lane == 1, pltpu.roll(mid, 1, 1), ends)
    ends = jnp.where(lane == 2, pltpu.roll(low, 2, 1), ends)
    kin = jnp.dot(t["family"][...], ends.astype(BF16), preferred_element_type=F32)
    up, down = kin[:nodes], kin[nodes:]
    up = up + pltpu.roll(up, 1, 1) + pltpu.roll(up, 2, 1)
    down = down + pltpu.roll(down, last, 1) + pltpu.roll(down, last - 1, 1)
    left = pltpu.roll(jnp.where(lane == last, up, purk), 1, 1)
    kinds = t["kinds"][...]
    left = jnp.where(jnp.logical_and(lane == 0, kinds > 0.0), purk, left)
    right = jnp.where(lane == last, purk, pltpu.roll(purk, last, 1))
    spread = left + right - 2.0 * purk
    extra = pltpu.roll(down, last, 1) - kinds * purk
    spread = spread + jnp.where(lane == last, extra, 0.0)
    purk_next = (
        purk
        + t["couple"][...] * spread
        + 0.2 * purk * (purk - 0.15) * (1.0 - purk)
        - 0.1 * rec
        - (t["node_gain"][...] * purk - drawn)
    )
    return purk_next, rec + 0.05 * (purk - 0.5 * rec)


TREE = ("family", "couple", "node_gain", "kinds")
BLOCK_VMEM = [
    pltpu.VMEM((8, 4, LANE, LANE), F32),
    pltpu.VMEM((8, LANE, 4 * LANE), BF16),
    pltpu.VMEM((8, ROWS_AT + 12 * BRICK, LANE), BF16),
]


def block_refs(hbm, vmem):
    blk = dict(zip("fsr", hbm))
    blk.update(zip(("f0", "s0", "r0"), vmem))
    return blk


def gate_kernel(par_ref, flag_ref, mem_ref, cy_ref, gate_ref, gate_out, source_out):
    m = [mem_ref[b] for b in range(OWN + 2)]
    source = gate_step(m, par_ref, flag_ref, cy_ref, gate_ref, gate_out)
    for b in range(OWN + 2):
        source_out[b] = source[b]


def first_kernel(
    flag_ref, mem_ref, source_ref, purk_ref, u_ref, w_ref, ic_ref, cg_ref, f_hbm, s_hbm, r_hbm,
    mem_out, msg_out, parts, f0, s0, r0, buf, sem1, sem2,
):
    nb = OWN + 2
    count = flag_ref[2]
    blk = block_refs((f_hbm, s_hbm, r_hbm), (f0, s0, r0))
    start_blocks(count, blk, sem1)
    parts[...] = wide2(purk_ref[...])
    m = [mem_ref[b] for b in range(nb)]
    wait_blocks(count, blk, sem1)
    early = sample(m, count, blk)
    add = inject(m, count, parts, cg_ref, blk)
    m = solve([source_ref[b] + add[b] for b in range(nb)], u_ref, w_ref, ic_ref)
    for b in range(nb):
        mem_out[b] = m[b]
    for copy in send(early, sample(m, count, blk), buf, msg_out, sem2):
        copy.wait()


def step_kernel(final, *refs):
    flag_ref, par_ref, gain_ref, mem_ref, source_ref, u_ref, w_ref, ic_ref, cg_ref, cy_ref = refs[:10]
    recv_hbm, sub_hbm, q_hbm, purk_hbm, rec_hbm = refs[10:15]
    tree_hbm = refs[15:19]
    blk_hbm = refs[19:22]
    rest = refs[22:]
    if final:
        mem_out, purk_out, rec_out = rest[:3]
        rest = rest[3:]
    else:
        gate_hbm, mem_out, purk_out, rec_out, gate_out, msg_out = rest[:6]
        rest = rest[6:]
    recv, hot_sub, hot_q, purk_buf, rec_buf, family, couple, node_gain, kinds = rest[:9]
    f0, s0, r0, parts, drawn, sem, sem1 = rest[9:16]
    if not final:
        gates, buf, sem2, sem3 = rest[16:]
    nb = OWN + 2
    count = flag_ref[2]
    blk = block_refs(blk_hbm, (f0, s0, r0))
    t = dict(zip(TREE, (family, couple, node_gain, kinds)))
    plan = [(recv_hbm, recv), (sub_hbm, hot_sub)]
    quarter = hot_q.shape[0] // 4
    for i in range(4):
        cut = pl.ds(i * quarter, quarter)
        plan.append((q_hbm.at[cut], hot_q.at[cut]))
    plan += [(purk_hbm, purk_buf), (rec_hbm, rec_buf)]
    plan += list(zip(tree_hbm, (family, couple, node_gain, kinds)))
    loads = [pltpu.make_async_copy(a, b, sem.at[k]) for k, (a, b) in enumerate(plan)]
    for load in loads:
        load.start()
    start_blocks(count, blk, sem1)
    gate_loads = []
    if not final:
        for i in range(nb // 2):
            cut = pl.ds(2 * i, 2)
            gate_loads.append(pltpu.make_async_copy(gate_hbm.at[cut], gates.at[cut], sem3.at[i]))
        for load in gate_loads:
            load.start()
    for load in loads[:2]:
        load.wait()
    to_nodes(arrange(recv, gain_ref), hot_sub, hot_q, drawn, loads[2:6])
    m = [mem_ref[b] for b in range(nb)]
    for load in loads[6:]:
        load.wait()
    wait_blocks(count, blk, sem1)
    purk, rec = purk_step(purk_buf[...], rec_buf[...], drawn[0], t)
    purk_buf[...] = purk
    rec_buf[...] = rec
    parts[...] = wide2(purk)
    add = inject(m, count, parts, cg_ref, blk)
    m = solve([source_ref[b] + add[b] for b in range(nb)], u_ref, w_ref, ic_ref)
    purk, rec = purk_step(purk_buf[...], rec_buf[...], drawn[1], t)
    purk_buf[...] = purk
    rec_buf[...] = rec
    stores = [
        pltpu.make_async_copy(purk_buf, purk_out, sem.at[0]),
        pltpu.make_async_copy(rec_buf, rec_out, sem.at[1]),
    ]
    for store in stores:
        store.start()
    if not final:
        parts[...] = wide2(purk)
        for load in gate_loads:
            load.wait()
        source = gate_step(m, par_ref, flag_ref, cy_ref, gates, gates)
        for i in range(nb // 2):
            cut = pl.ds(2 * i, 2)
            store = pltpu.make_async_copy(gates.at[cut], gate_out.at[cut], sem3.at[i])
            store.start()
            stores.append(store)
        early = sample(m, count, blk)
        add = inject(m, count, parts, cg_ref, blk)
        m = solve([source[b] + add[b] for b in range(nb)], u_ref, w_ref, ic_ref)
        stores += send(early, sample(m, count, blk), buf, msg_out, sem2)
    for b in range(nb):
        mem_out[b] = m[b]
    for store in stores:
        store.wait()


VMEM = pl.BlockSpec()
ANY = pl.BlockSpec(memory_space=pl.ANY)
SMEM = pl.BlockSpec(memory_space=pltpu.SMEM)


def shape(*dims):
    return jax.ShapeDtypeStruct(dims, F32)


def on_device(
    voltage,
    gates,
    couple_x,
    couple_y,
    gate_half,
    gate_slope,
    gate_rate,
    conductance,
    reversal,
    purk_volt,
    purk_recovery,
    purk_couple,
    parent,
    junc_purk,
    junc_cell,
    junc_owner,
    junc_gain,
):
    rows, cols = voltage.shape
    subs, seg = purk_volt.shape
    gz = lax.axis_size("gz")
    xy = lax.axis_size("xy")
    g = lax.axis_index("gz")
    x = lax.axis_index("xy")
    nvar = gates.shape[0]
    chunk = cols // gz
    wide = chunk + 2 * HALO
    total_rows = rows * gz
    nodes = parent.shape[0]
    nj = junc_gain.shape[0]
    slots = gz * CAP
    per_s = xy * slots

    owner = junc_owner[:, 0]
    same = owner[:, None] == owner[None, :]
    before = jnp.arange(nj)[:, None] > jnp.arange(nj)[None, :]
    rank = jnp.sum(jnp.logical_and(same, before).astype(jnp.int32), axis=1)
    slot = (owner % xy) * slots + (owner // xy) * CAP + rank
    hot = jnp.arange(per_s, dtype=jnp.int32)[:, None] == slot[None, :]

    def place(field):
        return jnp.sum(jnp.where(hot, field[None, :], 0.0), axis=1)

    table = jnp.stack(
        [place(junc_gain), place(junc_purk.astype(F32)), place(junc_cell.astype(F32))]
    )

    mine = jnp.concatenate(
        [purk_volt.reshape(-1, seg), purk_recovery.reshape(-1, seg), purk_couple.reshape(-1, seg), table.reshape(-1, seg)]
    )
    allp = lax.all_to_all(
        jnp.broadcast_to(mine[None], (xy,) + mine.shape), "xy", 0, 0, tiled=True
    )
    purk0 = allp[:, :subs].reshape(nodes, seg)
    rec0 = allp[:, subs : 2 * subs].reshape(nodes, seg)
    pcoup = allp[:, 2 * subs : 3 * subs].reshape(nodes, seg)
    tabs = allp[:, 3 * subs :].reshape(xy, 3, xy, slots)

    nb = gz + 2
    nf = nvar + 3

    def edge(at):
        cut = slice(at, at + chunk)
        return jnp.concatenate(
            [gates[:, :, cut], voltage[None, :, cut], couple_x[None, :, cut], couple_y[None, :, cut]]
        )

    left = lax.ppermute(edge(cols - chunk), "xy", [(i, i + 1) for i in range(xy - 1)])
    right = lax.ppermute(edge(0), "xy", [(i + 1, i) for i in range(xy - 1)])
    limit = pltpu.CompilerParams(vmem_limit_bytes=16 << 20)
    packed = pl.pallas_call(
        pack_kernel,
        out_shape=shape(gz, (nf + nvar // 4 + 1) * rows, chunk),
        compiler_params=limit,
        name="pack",
    )(gates, voltage, couple_x, couple_y, left, right)
    packed = lax.all_to_all(packed, "gz", 0, 0, tiled=True)
    slab_shape = shape(nb, rows, LANE)
    gate_shape = shape(nb, nvar, rows, LANE)
    flat = pltpu.VMEM((total_rows, LANE), F32)
    gate, mem, cy, gu, gw, ginv = pl.pallas_call(
        unpack_kernel,
        out_shape=(gate_shape,) + (slab_shape,) * 5,
        scratch_shapes=[flat] * 4,
        compiler_params=limit,
        name="unpack",
    )(packed)

    def side(which, shift):
        tab = lax.dynamic_index_in_dim(tabs, which, 2, keepdims=False)
        cell = tab[:, 2].reshape(xy, gz, CAP).astype(jnp.int32)
        purk = tab[:, 1].reshape(xy, gz, CAP).astype(jnp.int32)
        brick = jnp.arange(gz, dtype=jnp.int32)[None, :, None]
        row = brick * rows + cell // cols
        place_at = cell % cols + shift * cols - g * chunk + HALO
        sub = jnp.arange(xy, dtype=jnp.int32)[:, None, None] * subs + purk // seg
        return tuple(
            v.reshape(-1) for v in (tab[:, 0].reshape(xy, gz, CAP), row, place_at, sub, purk % seg)
        )

    gain_a, row_a, col_a, sub_a, q_a = side(x, 0)
    go_left = g == 0
    shift = jnp.where(go_left, -1, 1)
    other = x + shift
    near = jnp.logical_and(
        jnp.logical_or(go_left, g == gz - 1), jnp.logical_and(other >= 0, other < xy)
    )
    gain_b, row_b, col_b, sub_b, q_b = side(jnp.clip(other, 0, xy - 1), shift)
    gain_b = jnp.where(near, gain_b, 0.0)
    gain = jnp.concatenate([gain_a, gain_b])
    place_at = jnp.concatenate([col_a, col_b])
    number = jnp.arange(2 * per_s, dtype=jnp.int32)
    inside = jnp.logical_and(place_at >= HALO, place_at < HALO + chunk)
    sent = jnp.where(jnp.logical_and(inside, number < per_s), number, -1)
    fields = jnp.stack(
        [gain]
        + [
            v.astype(F32)
            for v in (
                jnp.concatenate([row_a, row_b]),
                place_at,
                jnp.concatenate([sub_a, sub_b]),
                jnp.concatenate([q_a, q_b]),
                sent,
            )
        ]
    )
    relevant = jnp.logical_and(
        gain > 0.0, jnp.logical_and(place_at >= 0, place_at < chunk + 2 * HALO)
    )
    until = jnp.cumsum(relevant.astype(jnp.int32))
    count = (until[-1] + LANE - 1) // LANE
    target = jnp.where(relevant, until - 1, -1)
    hot = (target[:, None] == number[None, :]).astype(BF16)
    got = jnp.dot(jnp.concatenate(cut3(fields)), hot, preferred_element_type=F32)
    nfield = fields.shape[0]
    packed_rows = got[:nfield] + got[nfield : 2 * nfield] + got[2 * nfield :]
    packed_cols = packed_rows.T
    alive = number < until[-1]

    def as_int(v):
        return v.astype(jnp.int32)

    gain_c = packed_cols[:, 0:1]
    row_c, col_c, sub_c, q_c, sent_c = (
        jnp.where(alive[:, None], as_int(packed_cols[:, i : i + 1]), -1) for i in range(1, 6)
    )
    row_r, sent_r = (jnp.where(alive, as_int(packed_rows[i]), -1) for i in (1, 5))
    lane = jnp.arange(LANE, dtype=jnp.int32)[None, :]
    wing_at = jnp.where(col_c < HALO, col_c, col_c - chunk)
    wing = jnp.logical_or(
        jnp.logical_and(col_c >= 0, col_c < HALO), col_c >= HALO + chunk
    )
    wing_at = jnp.where(wing, (row_c // rows % 4) * WING + wing_at, -1)
    t = {}
    t["gain_halo"] = jnp.where(wing_at == lane, gain_c, 0.0)
    t["gain_own"] = jnp.where(col_c - HALO == lane, gain_c, 0.0)
    t["q"] = (q_c == lane).astype(F32)
    t["slot_lane"] = (jnp.where(sent_c >= 0, sent_c % LANE, -1) == lane).astype(F32)
    t["row_t"] = (row_c == jnp.arange(total_rows)[None, :]).astype(BF16)
    t["sub"] = (sub_c == jnp.arange(nodes)[None, :]).astype(BF16)
    blocks = 2 * per_s // LANE
    row_b = row_r.reshape(blocks, 1, LANE)
    halo_row = (row_b // rows // 4) * rows + row_b % rows
    t["row"] = jnp.concatenate(
        [
            row_b == jnp.arange(total_rows)[None, :, None],
            jnp.logical_and(row_b >= 0, halo_row == jnp.arange(2 * rows)[None, :, None]),
        ],
        axis=1,
    ).astype(BF16)
    sent_b = sent_r.reshape(blocks, 1, LANE)
    t["slot_row"] = (
        jnp.where(sent_b >= 0, sent_b // LANE, -1) == jnp.arange(16)[None, :, None]
    ).astype(BF16)
    flat_row = jnp.transpose(t["row"], (1, 0, 2)).reshape(total_rows + 2 * rows, -1)
    cell_gain = jnp.concatenate(
        [
            hot_dot(flat_row[:total_rows], t["gain_own"]).reshape(gz, rows, LANE),
            hot_dot(flat_row[total_rows:], t["gain_halo"]).reshape(2, rows, LANE),
        ]
    )

    def by_block(v):
        return v.reshape(blocks, LANE, v.shape[-1])

    blk_f = jnp.stack(
        [by_block(t[n]) for n in ("gain_halo", "gain_own", "q", "slot_lane")], axis=1
    )
    blk_s = by_block(t["sub"])
    row_t = jnp.pad(by_block(t["row_t"]), ((0, 0), (0, 0), (0, LANE - total_rows)))
    blk_r = jnp.concatenate([row_t, t["row"], t["slot_row"]], axis=1)

    gain_p = tabs[:, 0].reshape(4, 4, 4, LANE)
    gain_t = jnp.transpose(gain_p, (2, 1, 0, 3))
    gain_t = jnp.concatenate([gain_t, gain_t], axis=2)
    node_p = tabs[:, 1].reshape(xy, per_s).astype(jnp.int32)
    sub_p = (node_p // seg).reshape(xy, 4, 1, LANE)
    hot_sub_p = (sub_p == jnp.arange(subs, dtype=jnp.int32)[None, None, :, None]).astype(BF16)
    hot_q_p = ((node_p % seg)[:, :, None] == jnp.arange(seg)[None, None, :]).astype(BF16)
    tree = {"couple": pcoup}
    tree["node_gain"] = pl.pallas_call(
        node_gain_kernel,
        out_shape=shape(nodes, seg),
        scratch_shapes=[pltpu.VMEM((2, nodes, seg), F32)],
        name="node_gain",
    )(gain_t, hot_sub_p, hot_q_p)
    all_ids = jnp.arange(nodes, dtype=jnp.int32)
    parent_hot = (all_ids[None, :] == parent[:, None]).astype(BF16)
    child_hot = (parent[None, :] == all_ids[:, None]).astype(BF16)
    tree["family"] = jnp.concatenate([parent_hot, child_hot])
    children = jnp.sum(child_hot.astype(F32), axis=1, keepdims=True)
    is_root = (parent < 0).astype(F32)[:, None]
    tree["kinds"] = jnp.where(lane == 0, is_root, jnp.where(lane == seg - 1, children, 0.0))

    par = jnp.stack(
        [
            0.5 * gate_slope,
            0.5 * gate_slope * gate_half,
            jnp.exp(-gate_rate),
            -0.5 * jnp.expm1(-gate_rate),
            conductance,
            conductance * reversal,
        ]
    )
    flags = jnp.stack(
        [
            jnp.logical_and(x == 0, g == 0).astype(jnp.int32),
            jnp.logical_and(x == xy - 1, g == gz - 1).astype(jnp.int32),
            count.astype(jnp.int32),
        ]
    )
    blks, tree, gain_t, hot_sub_p, hot_q_p, cell_gain = lax.optimization_barrier(
        ([blk_f, blk_s, blk_r], [tree[n] for n in TREE], gain_t, hot_sub_p, hot_q_p, cell_gain)
    )
    node_shape = shape(nodes, seg)
    msg_shape = shape(gz * xy, 8, LANE)
    parts = pltpu.VMEM((nodes, 2 * LANE), BF16)
    drawn = pltpu.VMEM((2, nodes, seg), F32)
    send_buf = pltpu.VMEM((16, 8, LANE), F32)
    dma = pltpu.SemaphoreType.DMA
    solver = [gu, gw, ginv, cell_gain]
    limit = pltpu.CompilerParams(vmem_limit_bytes=24 << 20)

    def gate_call(mem, gate):
        return pl.pallas_call(
            gate_kernel,
            out_shape=(gate_shape, slab_shape),
            in_specs=[SMEM, SMEM, VMEM, VMEM, VMEM],
            out_specs=(VMEM, VMEM),
            input_output_aliases={4: 0},
            compiler_params=limit,
            cost_estimate=pl.CostEstimate(flops=8_000_000, transcendentals=900_000, bytes_accessed=3_400_000),
            name="gate",
        )(par, flags, mem, cy, gate)

    def exchange(msg):
        got = lax.all_to_all(msg, ("gz", "xy"), 0, 0, tiled=True)
        return got.reshape(gz, xy, 8, LANE)

    def step_call(final, recv, mem, source, purk, rec, gate):
        args = [flags, par, gain_t, mem, source] + solver + [cy]
        args += [recv, hot_sub_p, hot_q_p, purk, rec] + tree + blks
        specs = [SMEM, SMEM] + [VMEM] * 8 + [ANY] * 12
        outs = [slab_shape, node_shape, node_shape]
        out_specs = [VMEM, ANY, ANY]
        alias = {3: 0, 13: 1, 14: 2}
        scratch = [
            pltpu.VMEM(recv.shape, F32),
            pltpu.VMEM(hot_sub_p.shape, BF16),
            pltpu.VMEM(hot_q_p.shape, BF16),
            pltpu.VMEM((nodes, seg), F32),
            pltpu.VMEM((nodes, seg), F32),
            pltpu.VMEM((2 * nodes, nodes), BF16),
        ]
        scratch += [pltpu.VMEM((nodes, seg), F32)] * 3 + BLOCK_VMEM
        scratch += [parts, drawn, dma((12,)), dma((3, 8))]
        if not final:
            args += [gate]
            specs += [ANY]
            outs += [gate_shape, msg_shape]
            out_specs += [ANY, ANY]
            alias[22] = 3
            scratch += [pltpu.VMEM((nb, nvar, rows, LANE), F32), send_buf, dma((8,)), dma((5,))]
        return pl.pallas_call(
            lambda *refs: step_kernel(final, *refs),
            out_shape=tuple(outs),
            in_specs=specs,
            out_specs=tuple(out_specs),
            scratch_shapes=scratch,
            input_output_aliases=alias,
            compiler_params=limit,
            name="last" if final else "step",
        )(*args)

    gate, source = gate_call(mem, gate)
    mem, msg = pl.pallas_call(
        first_kernel,
        out_shape=(slab_shape, msg_shape),
        in_specs=[SMEM] + [VMEM] * 7 + [ANY] * 3,
        out_specs=(VMEM, ANY),
        scratch_shapes=[parts] + BLOCK_VMEM + [send_buf, dma((3, 8)), dma((8,))],
        compiler_params=limit,
        name="first",
    )(flags, mem, source, purk0, *solver, *blks)

    def two(k, state):
        mem, gate, purk, rec, msg = state
        recv = exchange(msg)
        gate, source = gate_call(mem, gate)
        mem, purk, rec, gate, msg = step_call(False, recv, mem, source, purk, rec, gate)
        return mem, gate, purk, rec, msg

    mem, gate, purk, rec, msg = lax.fori_loop(
        0, STEPS // 2 - 1, two, (mem, gate, purk0, rec0, msg)
    )
    recv = exchange(msg)
    gate, source = gate_call(mem, gate)

    mem, purk, rec = step_call(True, recv, mem, source, purk, rec, gate)

    back = jnp.concatenate([gate[:gz], mem[:gz, None]], axis=1).reshape(gz, -1, chunk)
    back = lax.all_to_all(back, "gz", 0, 0, tiled=True)
    back = back.reshape(gz, nvar + 1, rows, chunk)
    back = jnp.transpose(back, (1, 2, 0, 3)).reshape(nvar + 1, rows, cols)
    purk_mine = lax.dynamic_slice_in_dim(purk, x * subs, subs, axis=0)
    rec_mine = lax.dynamic_slice_in_dim(rec, x * subs, subs, axis=0)
    return back[nvar], back[:nvar], purk_mine, rec_mine


def solution(mesh):
    return jax.shard_map(
        on_device,
        mesh=mesh,
        in_specs=(
            P("gz", "xy"),
            P(None, "gz", "xy"),
            P("gz", "xy"),
            P("gz", "xy"),
            P(),
            P(),
            P(),
            P(),
            P(),
            P("xy", None),
            P("xy", None),
            P("xy", None),
            P(),
            P("xy"),
            P("xy"),
            P("xy", None),
            P("xy"),
        ),
        out_specs=(P("gz", "xy"), P(None, "gz", "xy"), P("xy", None), P("xy", None)),
        check_vma=False,
    )
```

```python
import jax
import jax.numpy as jnp
from jax import lax
from jax.experimental import pallas as pl
from jax.experimental.pallas import tpu as pltpu
from jax.sharding import PartitionSpec as P

STEPS = 16
HALO = 16
CAP = 4
OWN = 8
BRICK = 8
LANE = 128
WING = 32
ROWS_AT = 128
F32 = jnp.float32
BF16 = jnp.bfloat16


def split3(value):
    high = value.astype(BF16)
    rest = value - high.astype(F32)
    mid = rest.astype(BF16)
    low = (rest - mid.astype(F32)).astype(BF16)
    return high, mid, low


def cut3(value):
    high = lax.reduce_precision(value, 8, 7)
    rest = value - high
    mid = lax.reduce_precision(rest, 8, 7)
    return high.astype(BF16), mid.astype(BF16), (rest - mid).astype(BF16)


def hot_dot(hot, value):
    parts = jnp.concatenate(cut3(value), axis=-1)
    got = jnp.dot(hot, parts, preferred_element_type=F32)
    n = value.shape[-1]
    return got[..., :n] + got[..., n : 2 * n] + got[..., 2 * n :]


def table_kernel(field_ref, volt_ref, rec_ref, couple_ref, out_ref):
    fields = field_ref[...]
    nj = fields.shape[1]
    xy = out_ref.shape[0]
    own_row = fields[3:4, :]
    first = lax.broadcasted_iota(jnp.int32, (nj, nj), 0)
    second = lax.broadcasted_iota(jnp.int32, (nj, nj), 1)
    own_col = jnp.sum(jnp.where(first == second, own_row, 0.0), axis=1, keepdims=True)
    earlier = jnp.logical_and(own_col == own_row, first < second)
    rank = jnp.sum(jnp.where(earlier, 1.0, 0.0), axis=0, keepdims=True)
    high = jnp.floor(own_row * (1.0 / xy))
    slot = (own_row - high * xy) * (OWN * CAP) + high * CAP + rank
    slots = xy * OWN * CAP
    at = lax.broadcasted_iota(jnp.int32, (slots, nj), 0)
    hot = jnp.where(at == slot.astype(jnp.int32), 1.0, 0.0).astype(BF16)
    parts = jnp.concatenate([v.astype(F32) for v in split3(fields)], axis=0).astype(BF16)
    got = lax.dot_general(parts, hot, (((1,), (1,)), ((), ())), preferred_element_type=F32)
    n = fields.shape[0]
    got = got[:n] + got[n : 2 * n] + got[2 * n :]
    subs = volt_ref.shape[0]
    span = slots // LANE
    rows = [got[f : f + 1, k * LANE : (k + 1) * LANE] for f in range(3) for k in range(span)]
    for i in range(xy):
        out_ref[i, :subs, :] = volt_ref[...]
        out_ref[i, subs : 2 * subs, :] = rec_ref[...]
        out_ref[i, 2 * subs : 3 * subs, :] = couple_ref[...]
        for r, row in enumerate(rows):
            out_ref[i, 3 * subs + r : 3 * subs + r + 1, :] = row


def pack_kernel(gate_ref, volt_ref, cx_ref, cy_ref, left_ref, right_ref, out_ref):
    lane = lanes()
    nvar = gate_ref.shape[0]
    fields = nvar + 3
    chunks = out_ref.shape[0]
    extra = (volt_ref, cx_ref, cy_ref)
    span = [slice(g * LANE, (g + 1) * LANE) for g in range(chunks)]

    def put(f4, pick, count):
        for fl in range(count):
            at = pl.ds(pl.multiple_of((f4 * 4 + fl) * BRICK, BRICK), BRICK)
            for g in range(chunks):
                out_ref[g, at, :] = pick(fl, g)
        at = pl.ds(pl.multiple_of((fields + f4) * BRICK, BRICK), BRICK)
        for g in range(chunks):
            v = jnp.zeros((BRICK, LANE), F32)
            for fl in range(count):
                base = fl * WING
                low = pltpu.roll(pick(fl, g - 1), (base + HALO) % LANE, 1)
                high = pltpu.roll(pick(fl, g + 1), (base + HALO) % LANE, 1)
                v = jnp.where(jnp.logical_and(lane >= base, lane < base + HALO), low, v)
                v = jnp.where(jnp.logical_and(lane >= base + HALO, lane < base + WING), high, v)
            out_ref[g, at, :] = v

    def body(f4, carried):
        def pick(fl, g):
            f = f4 * 4 + fl
            if g < 0:
                return left_ref[f]
            return right_ref[f] if g == chunks else gate_ref[f, :, span[g]]

        put(f4, pick, 4)
        return carried

    lax.fori_loop(0, nvar // 4, body, 0)

    def pick(fl, g):
        if g < 0:
            return left_ref[nvar + fl]
        return right_ref[nvar + fl] if g == chunks else extra[fl][:, span[g]]

    put(nvar // 4, pick, 3)


def unpack_kernel(in_ref, gate_ref, mem_ref, cy_ref, u_ref, w_ref, ic_ref, near, u_far, w_far, i_far):
    nvar = gate_ref.shape[1]
    fields = nvar + 3
    group = lanes() // WING
    total = OWN * BRICK

    def gather(piece, h, fl):
        v = None
        for lg in range(4):
            part = piece(h * 4 + lg)
            if lg != fl:
                part = pltpu.roll(part, ((lg - fl) * WING) % LANE, 1)
            v = part if v is None else jnp.where(group == lg, part, v)
        return v

    def body(f4, carried):
        at = pl.ds(pl.multiple_of((fields + f4) * BRICK, BRICK), BRICK)
        for fl in range(4):
            f = f4 * 4 + fl
            own = pl.ds(pl.multiple_of(f * BRICK, BRICK), BRICK)
            for b in range(OWN):
                gate_ref[b, f] = in_ref[b, own, :]
            for h in range(2):
                gate_ref[OWN + h, f] = gather(lambda b: in_ref[b, at, :], h, fl)
        return carried

    lax.fori_loop(0, nvar // 4, body, 0)
    tail = slice((fields + nvar // 4) * BRICK, (fields + nvar // 4 + 1) * BRICK)
    for b in range(OWN):
        mem_ref[b] = in_ref[b, nvar * BRICK : (nvar + 1) * BRICK, :]
        cy_ref[b] = in_ref[b, (nvar + 2) * BRICK : (nvar + 3) * BRICK, :]
        c = in_ref[b, (nvar + 1) * BRICK : (nvar + 2) * BRICK, :]
        inv = 1.0 / c
        ic_ref[b] = inv
        near[b * BRICK : (b + 1) * BRICK, :] = inv
        c = in_ref[b, tail, :]
        i_far[b * BRICK : (b + 1) * BRICK, :] = 1.0 / jnp.where(c > 1.0, c, 300.0)
    for h in range(2):
        mem_ref[OWN + h] = gather(lambda b: in_ref[b, tail, :], h, 0)
        cy_ref[OWN + h] = gather(lambda b: in_ref[b, tail, :], h, 2)

    def put_u(i, one, two):
        u_ref[i // BRICK, i % BRICK : i % BRICK + 1, :] = one
        u_far[i : i + 1, :] = two

    def put_w(i, one, two):
        w_ref[i // BRICK, i % BRICK : i % BRICK + 1, :] = one
        w_far[i : i + 1, :] = two

    def both(i):
        return near[i : i + 1, :], i_far[i : i + 1, :]

    u = [jnp.ones((1, LANE), F32)] * 2
    d = [jnp.zeros((1, LANE), F32)] * 2
    put_u(0, *u)
    for i in range(total - 1):
        inv = both(i)
        d = [d[n] + u[n] * inv[n] for n in range(2)]
        u = [u[n] + d[n] for n in range(2)]
        put_u(i + 1, *u)
    inv = both(total - 1)
    e = list(inv)
    scale = [1.0 / (d[n] * (1.0 + e[n]) + (u[n] - d[n]) * e[n]) for n in range(2)]
    w = [jnp.ones((1, LANE), F32)] * 2
    put_w(total - 1, *(w[n] * scale[n] for n in range(2)))
    w = [w[n] + e[n] for n in range(2)]
    put_w(total - 2, *(w[n] * scale[n] for n in range(2)))
    for i in range(total - 2, 0, -1):
        inv = both(i)
        e = [e[n] + w[n] * inv[n] for n in range(2)]
        w = [w[n] + e[n] for n in range(2)]
        put_w(i - 1, *(w[n] * scale[n] for n in range(2)))
    for far, out_ref in ((u_far, u_ref), (w_far, w_ref), (i_far, ic_ref)):
        for h in range(2):
            out_ref[OWN + h] = gather(lambda b: far[b * BRICK : (b + 1) * BRICK, :], h, 1)


def lanes():
    return lax.broadcasted_iota(jnp.int32, (BRICK, LANE), 1)


def sublanes():
    return lax.broadcasted_iota(jnp.int32, (BRICK, LANE), 0)


def wide2(value):
    high = value.astype(BF16)
    return jnp.concatenate([high, (value - high.astype(F32)).astype(BF16)], axis=1)


def fold2(value):
    return value[:, :LANE] + value[:, LANE:]


def neighbours(m, at_left, at_right):
    lane = lanes()
    c = lane % WING
    left, right = [], []
    for b in range(OWN):
        h, base = OWN + b // 4, (b % 4) * WING
        edge = pltpu.roll(m[h], (LANE - (base + HALO - 1)) % LANE, 1)
        edge = jnp.where(at_left, m[b], edge)
        left.append(jnp.where(lane == 0, edge, pltpu.roll(m[b], 1, 1)))
        edge = pltpu.roll(m[h], (LANE - 1 - (base + HALO)) % LANE, 1)
        edge = jnp.where(at_right, m[b], edge)
        right.append(jnp.where(lane == LANE - 1, edge, pltpu.roll(m[b], LANE - 1, 1)))
    for h in range(2):
        v = m[OWN + h]
        lf = jnp.where(c == 0, v, pltpu.roll(v, 1, 1))
        rt = jnp.where(c == WING - 1, v, pltpu.roll(v, LANE - 1, 1))
        for k in range(4):
            own, base = m[h * 4 + k], k * WING
            lf = jnp.where(lane == base + HALO, pltpu.roll(own, (base + HALO + 1) % LANE, 1), lf)
            rt = jnp.where(lane == base + HALO - 1, pltpu.roll(own, (base + HALO - 1) % LANE, 1), rt)
        left.append(lf)
        right.append(rt)
    return left, right


def gate_step(m, par_ref, flag_ref, cy_ref, gate_in, gate_out):
    zero = jnp.zeros((BRICK, LANE), F32)
    nb = OWN + 2

    def body(k, carried):
        total, push = carried
        slope, offset, decay = par_ref[0, k], par_ref[1, k], par_ref[2, k]
        grow, weight, driven = par_ref[3, k], par_ref[4, k], par_ref[5, k]
        total_next, push_next = [], []
        for b in range(nb):
            bend = jnp.tanh(m[b] * slope - offset)
            gate = (gate_in[b, k] * decay + grow) + grow * bend
            gate_out[b, k] = gate
            total_next.append(total[b] + weight * gate)
            push_next.append(push[b] + driven * gate)
        return tuple(total_next), tuple(push_next)

    start = (tuple([zero] * nb), tuple([zero] * nb))
    total, push = lax.fori_loop(0, gate_in.shape[1], body, start, unroll=8)
    left, right = neighbours(m, flag_ref[0] > 0, flag_ref[1] > 0)
    return [
        m[b] - (m[b] * total[b] - push[b]) + cy_ref[b] * (left[b] + right[b] - 2.0 * m[b])
        for b in range(nb)
    ]


def solve(source, u_ref, w_ref, ic_ref):
    row, lane = sublanes(), lanes()
    nb = OWN + 2
    before, after, total_b, total_a = [], [], [], []
    for b in range(nb):
        s = source[b] * ic_ref[b]
        p = u_ref[b] * s
        q = w_ref[b] * s
        for step in (1, 2, 4):
            p = p + jnp.where(row >= step, pltpu.roll(p, step, 0), 0.0)
            q = q + jnp.where(row < BRICK - step, pltpu.roll(q, BRICK - step, 0), 0.0)
        total_b.append(jnp.broadcast_to(p[BRICK - 1 : BRICK, :], p.shape))
        total_a.append(jnp.broadcast_to(q[0:1, :], q.shape))
        before.append(p)
        after.append(jnp.where(row < BRICK - 1, pltpu.roll(q, BRICK - 1, 0), 0.0))
    run = None
    for b in range(OWN):
        if run is not None:
            before[b] = before[b] + run
        run = total_b[b] if run is None else run + total_b[b]
    run = None
    for b in range(OWN - 1, -1, -1):
        if run is not None:
            after[b] = after[b] + run
        run = total_a[b] if run is None else run + total_a[b]

    def scan4(t, up):
        shift = (lambda v, n: pltpu.roll(v, n, 1)) if up else (lambda v, n: pltpu.roll(v, LANE - n, 1))
        ok = (lambda n: lane >= n) if up else (lambda n: lane < LANE - n)
        one = t + jnp.where(ok(WING), shift(t, WING), 0.0)
        two = one + jnp.where(ok(2 * WING), shift(one, 2 * WING), 0.0)
        return jnp.where(ok(WING), shift(two, WING), 0.0)

    def all4(t):
        two = t + pltpu.roll(t, WING, 1)
        return two + pltpu.roll(two, 2 * WING, 1)

    before[OWN] = before[OWN] + scan4(total_b[OWN], True)
    before[OWN + 1] = before[OWN + 1] + scan4(total_b[OWN + 1], True) + all4(total_b[OWN])
    after[OWN + 1] = after[OWN + 1] + scan4(total_a[OWN + 1], False)
    after[OWN] = after[OWN] + scan4(total_a[OWN], False) + all4(total_a[OWN + 1])
    return [w_ref[b] * before[b] + u_ref[b] * after[b] for b in range(nb)]


def over_blocks(count, blk, use, start):
    def body(b, carried):
        return use(blk["f0"].at[b], blk["s0"].at[b], blk["r0"].at[b], carried)

    return lax.fori_loop(0, count, body, start)


def block_copies(b, blk, sem):
    return [
        pltpu.make_async_copy(blk[n].at[b], blk[n + "0"].at[b], sem.at[k, b])
        for k, n in enumerate("fsr")
    ]


def start_blocks(count, blk, sem):
    def body(b, carried):
        for copy in block_copies(b, blk, sem):
            copy.start()
        return carried

    lax.fori_loop(0, count, body, 0)


def wait_blocks(count, blk, sem):
    def body(b, carried):
        for copy in block_copies(b, blk, sem):
            copy.wait()
        return carried

    lax.fori_loop(0, count, body, 0)


def sample(m, count, blk):
    rows = jnp.concatenate(m[:OWN], axis=0)
    big = wide2(jnp.concatenate([rows, jnp.zeros_like(rows)], axis=0))

    def use(f, s, r, msg):
        picked = fold2(jnp.dot(r[:LANE, :], big, preferred_element_type=F32))
        picked = jnp.where(f[1] > 0.0, picked, 0.0)
        value = jnp.sum(picked, axis=1, keepdims=True)
        value = wide2(value * f[3])
        slot_row = r[ROWS_AT + 10 * BRICK : ROWS_AT + 12 * BRICK, :]
        return msg + fold2(jnp.dot(slot_row, value, preferred_element_type=F32))

    return over_blocks(count, blk, use, jnp.zeros((2 * BRICK, LANE), F32))


def send(early, late, buf, msg_out, sem):
    both = jnp.concatenate([early[:4], late[:4]], axis=0)
    n = buf.shape[0]
    for i in range(n):
        buf[i] = both
    copies = [
        pltpu.make_async_copy(buf, msg_out.at[pl.ds(i * n, n)], sem.at[i])
        for i in range(msg_out.shape[0] // n)
    ]
    for copy in copies:
        copy.start()
    return copies


def inject(m, count, purk_parts, cell_gain, blk):
    nr = OWN * BRICK

    def use(f, s, r, carried):
        own, halo = carried
        got = fold2(jnp.dot(s[...], purk_parts[...], preferred_element_type=F32))
        volts = jnp.sum(got * f[2], axis=1, keepdims=True)
        own = own + fold2(
            jnp.dot(r[ROWS_AT : ROWS_AT + nr, :], wide2(volts * f[1]), preferred_element_type=F32)
        )
        halo = halo + fold2(
            jnp.dot(
                r[ROWS_AT + nr : ROWS_AT + nr + 2 * BRICK, :],
                wide2(volts * f[0]),
                preferred_element_type=F32,
            )
        )
        return own, halo

    start = (jnp.zeros((nr, LANE), F32), jnp.zeros((2 * BRICK, LANE), F32))
    own, halo = over_blocks(count, blk, use, start)
    parts = [own[b * BRICK : (b + 1) * BRICK] for b in range(OWN)]
    parts += [halo[:BRICK], halo[BRICK:]]
    return [parts[b] - cell_gain[b] * m[b] for b in range(OWN + 2)]


def to_nodes(tile, hot_sub, hot_q, out_ref, waits=()):
    subs = hot_sub.shape[2]
    for s in range(hot_q.shape[0]):
        if waits and s % 4 == 0:
            waits[s // 4].wait()
        rows = []
        for time in range(2):
            high, low = [], []
            for xh in range(4):
                r = tile[xh][s % 4][time * 4 + s // 4 : time * 4 + s // 4 + 1, :]
                hot = hot_sub[s, xh]
                up = r.astype(BF16).astype(F32)
                high.append(hot * jnp.broadcast_to(up, (subs, LANE)).astype(BF16))
                low.append(hot * jnp.broadcast_to(r - up, (subs, LANE)).astype(BF16))
            rows += [jnp.concatenate(high, axis=1), jnp.concatenate(low, axis=1)]
        got = jnp.dot(jnp.concatenate(rows, axis=0), hot_q[s], preferred_element_type=F32)
        out_ref[0, s * subs : (s + 1) * subs, :] = got[:subs] + got[subs : 2 * subs]
        out_ref[1, s * subs : (s + 1) * subs, :] = got[2 * subs : 3 * subs] + got[3 * subs :]


def node_gain_kernel(gain_ref, hot_sub, hot_q, out_ref, both):
    tile = [[gain_ref[xh, a] for a in range(4)] for xh in range(4)]
    to_nodes(tile, hot_sub, hot_q, both)
    out_ref[...] = both[0]


def arrange(recv_ref, gain_ref):
    group = lanes() // WING
    summed = []
    for x in range(recv_ref.shape[1]):
        v = recv_ref[0, x]
        for g in range(1, recv_ref.shape[0]):
            v = v + recv_ref[g, x]
        summed.append(v)
    tile = []
    for xh in range(4):
        row = []
        for a in range(4):
            v = None
            for b in range(4):
                piece = summed[xh * 4 + b]
                if a != b:
                    piece = pltpu.roll(piece, ((b - a) * WING) % LANE, 1)
                v = piece if v is None else jnp.where(group == b, piece, v)
            row.append(v * gain_ref[xh, a])
        tile.append(row)
    return tile


def purk_step(purk, rec, drawn, t):
    nodes = purk.shape[0]
    lane = lax.broadcasted_iota(jnp.int32, purk.shape, 1)
    high, mid, low = (v.astype(F32) for v in split3(purk))
    last = LANE - 1
    ends = jnp.where(lane == last, high, 0.0) + jnp.where(lane == 0, high, 0.0)
    ends = jnp.where(lane == last - 1, pltpu.roll(mid, last, 1), ends)
    ends = jnp.where(lane == last - 2, pltpu.roll(low, last - 1, 1), ends)
    ends = jnp.where(lane == 1, pltpu.roll(mid, 1, 1), ends)
    ends = jnp.where(lane == 2, pltpu.roll(low, 2, 1), ends)
    kin = jnp.dot(t["family"][...], ends.astype(BF16), preferred_element_type=F32)
    up, down = kin[:nodes], kin[nodes:]
    up = up + pltpu.roll(up, 1, 1) + pltpu.roll(up, 2, 1)
    down = down + pltpu.roll(down, last, 1) + pltpu.roll(down, last - 1, 1)
    left = pltpu.roll(jnp.where(lane == last, up, purk), 1, 1)
    kinds = t["kinds"][...]
    left = jnp.where(jnp.logical_and(lane == 0, kinds > 0.0), purk, left)
    right = jnp.where(lane == last, purk, pltpu.roll(purk, last, 1))
    spread = left + right - 2.0 * purk
    extra = pltpu.roll(down, last, 1) - kinds * purk
    spread = spread + jnp.where(lane == last, extra, 0.0)
    purk_next = (
        purk
        + t["couple"][...] * spread
        + 0.2 * purk * (purk - 0.15) * (1.0 - purk)
        - 0.1 * rec
        - (t["node_gain"][...] * purk - drawn)
    )
    return purk_next, rec + 0.05 * (purk - 0.5 * rec)


TREE = ("family", "couple", "node_gain", "kinds")
BLOCK_VMEM = [
    pltpu.VMEM((8, 4, LANE, LANE), F32),
    pltpu.VMEM((8, LANE, 4 * LANE), BF16),
    pltpu.VMEM((8, ROWS_AT + 12 * BRICK, LANE), BF16),
]


def block_refs(hbm, vmem):
    blk = dict(zip("fsr", hbm))
    blk.update(zip(("f0", "s0", "r0"), vmem))
    return blk


def gate_kernel(par_ref, flag_ref, mem_ref, cy_ref, gate_ref, gate_out, source_out):
    m = [mem_ref[b] for b in range(OWN + 2)]
    source = gate_step(m, par_ref, flag_ref, cy_ref, gate_ref, gate_out)
    for b in range(OWN + 2):
        source_out[b] = source[b]


def first_kernel(
    flag_ref, mem_ref, source_ref, purk_ref, u_ref, w_ref, ic_ref, cg_ref, f_hbm, s_hbm, r_hbm,
    mem_out, msg_out, parts, f0, s0, r0, buf, sem1, sem2,
):
    nb = OWN + 2
    count = flag_ref[2]
    blk = block_refs((f_hbm, s_hbm, r_hbm), (f0, s0, r0))
    start_blocks(count, blk, sem1)
    parts[...] = wide2(purk_ref[...])
    m = [mem_ref[b] for b in range(nb)]
    wait_blocks(count, blk, sem1)
    early = sample(m, count, blk)
    add = inject(m, count, parts, cg_ref, blk)
    m = solve([source_ref[b] + add[b] for b in range(nb)], u_ref, w_ref, ic_ref)
    for b in range(nb):
        mem_out[b] = m[b]
    for copy in send(early, sample(m, count, blk), buf, msg_out, sem2):
        copy.wait()


def step_kernel(final, *refs):
    flag_ref, par_ref, gain_ref, mem_ref, source_ref, u_ref, w_ref, ic_ref, cg_ref, cy_ref = refs[:10]
    recv_hbm, sub_hbm, q_hbm, purk_hbm, rec_hbm = refs[10:15]
    tree_hbm = refs[15:19]
    blk_hbm = refs[19:22]
    rest = refs[22:]
    if final:
        mem_out, purk_out, rec_out = rest[:3]
        rest = rest[3:]
    else:
        gate_hbm, mem_out, purk_out, rec_out, gate_out, msg_out = rest[:6]
        rest = rest[6:]
    recv, hot_sub, hot_q, purk_buf, rec_buf, family, couple, node_gain, kinds = rest[:9]
    f0, s0, r0, parts, drawn, sem, sem1 = rest[9:16]
    if not final:
        gates, buf, sem2, sem3 = rest[16:]
    nb = OWN + 2
    count = flag_ref[2]
    blk = block_refs(blk_hbm, (f0, s0, r0))
    t = dict(zip(TREE, (family, couple, node_gain, kinds)))
    plan = [(recv_hbm, recv), (sub_hbm, hot_sub)]
    quarter = hot_q.shape[0] // 4
    for i in range(4):
        cut = pl.ds(i * quarter, quarter)
        plan.append((q_hbm.at[cut], hot_q.at[cut]))
    plan += [(purk_hbm, purk_buf), (rec_hbm, rec_buf)]
    plan += list(zip(tree_hbm, (family, couple, node_gain, kinds)))
    loads = [pltpu.make_async_copy(a, b, sem.at[k]) for k, (a, b) in enumerate(plan)]
    for load in loads:
        load.start()
    start_blocks(count, blk, sem1)
    gate_loads = []
    if not final:
        for i in range(nb // 2):
            cut = pl.ds(2 * i, 2)
            gate_loads.append(pltpu.make_async_copy(gate_hbm.at[cut], gates.at[cut], sem3.at[i]))
        for load in gate_loads:
            load.start()
    for load in loads[:2]:
        load.wait()
    to_nodes(arrange(recv, gain_ref), hot_sub, hot_q, drawn, loads[2:6])
    m = [mem_ref[b] for b in range(nb)]
    for load in loads[6:]:
        load.wait()
    wait_blocks(count, blk, sem1)
    purk, rec = purk_step(purk_buf[...], rec_buf[...], drawn[0], t)
    purk_buf[...] = purk
    rec_buf[...] = rec
    parts[...] = wide2(purk)
    add = inject(m, count, parts, cg_ref, blk)
    m = solve([source_ref[b] + add[b] for b in range(nb)], u_ref, w_ref, ic_ref)
    purk, rec = purk_step(purk_buf[...], rec_buf[...], drawn[1], t)
    purk_buf[...] = purk
    rec_buf[...] = rec
    stores = [
        pltpu.make_async_copy(purk_buf, purk_out, sem.at[0]),
        pltpu.make_async_copy(rec_buf, rec_out, sem.at[1]),
    ]
    for store in stores:
        store.start()
    if not final:
        parts[...] = wide2(purk)
        for load in gate_loads:
            load.wait()
        source = gate_step(m, par_ref, flag_ref, cy_ref, gates, gates)
        for i in range(nb // 2):
            cut = pl.ds(2 * i, 2)
            store = pltpu.make_async_copy(gates.at[cut], gate_out.at[cut], sem3.at[i])
            store.start()
            stores.append(store)
        early = sample(m, count, blk)
        add = inject(m, count, parts, cg_ref, blk)
        m = solve([source[b] + add[b] for b in range(nb)], u_ref, w_ref, ic_ref)
        stores += send(early, sample(m, count, blk), buf, msg_out, sem2)
    for b in range(nb):
        mem_out[b] = m[b]
    for store in stores:
        store.wait()


VMEM = pl.BlockSpec()
ANY = pl.BlockSpec(memory_space=pl.ANY)
SMEM = pl.BlockSpec(memory_space=pltpu.SMEM)


def shape(*dims):
    return jax.ShapeDtypeStruct(dims, F32)


def on_device(
    voltage,
    gates,
    couple_x,
    couple_y,
    gate_half,
    gate_slope,
    gate_rate,
    conductance,
    reversal,
    purk_volt,
    purk_recovery,
    purk_couple,
    parent,
    junc_purk,
    junc_cell,
    junc_owner,
    junc_gain,
):
    rows, cols = voltage.shape
    subs, seg = purk_volt.shape
    gz = lax.axis_size("gz")
    xy = lax.axis_size("xy")
    g = lax.axis_index("gz")
    x = lax.axis_index("xy")
    nvar = gates.shape[0]
    chunk = cols // gz
    wide = chunk + 2 * HALO
    total_rows = rows * gz
    nodes = parent.shape[0]
    nj = junc_gain.shape[0]
    slots = gz * CAP
    per_s = xy * slots

    fields = jnp.stack(
        [junc_gain]
        + [v.astype(F32) for v in (junc_purk, junc_cell, junc_owner[:, 0])]
        + [jnp.zeros_like(junc_gain)] * 4
    )
    mine = pl.pallas_call(
        table_kernel,
        out_shape=shape(xy, 3 * subs + 3 * per_s // seg, seg),
        name="table",
    )(fields, purk_volt, purk_recovery, purk_couple)
    allp = lax.all_to_all(mine, "xy", 0, 0, tiled=True)
    purk0 = allp[:, :subs].reshape(nodes, seg)
    rec0 = allp[:, subs : 2 * subs].reshape(nodes, seg)
    pcoup = allp[:, 2 * subs : 3 * subs].reshape(nodes, seg)
    tabs = allp[:, 3 * subs :].reshape(xy, 3, xy, slots)

    nb = gz + 2
    nf = nvar + 3

    def edge(at):
        cut = slice(at, at + chunk)
        return jnp.concatenate(
            [gates[:, :, cut], voltage[None, :, cut], couple_x[None, :, cut], couple_y[None, :, cut]]
        )

    left = lax.ppermute(edge(cols - chunk), "xy", [(i, i + 1) for i in range(xy - 1)])
    right = lax.ppermute(edge(0), "xy", [(i + 1, i) for i in range(xy - 1)])
    limit = pltpu.CompilerParams(vmem_limit_bytes=16 << 20)
    packed = pl.pallas_call(
        pack_kernel,
        out_shape=shape(gz, (nf + nvar // 4 + 1) * rows, chunk),
        compiler_params=limit,
        name="pack",
    )(gates, voltage, couple_x, couple_y, left, right)
    packed = lax.all_to_all(packed, "gz", 0, 0, tiled=True)
    slab_shape = shape(nb, rows, LANE)
    gate_shape = shape(nb, nvar, rows, LANE)
    flat = pltpu.VMEM((total_rows, LANE), F32)
    gate, mem, cy, gu, gw, ginv = pl.pallas_call(
        unpack_kernel,
        out_shape=(gate_shape,) + (slab_shape,) * 5,
        scratch_shapes=[flat] * 4,
        compiler_params=limit,
        name="unpack",
    )(packed)

    def side(which, shift):
        tab = lax.dynamic_index_in_dim(tabs, which, 2, keepdims=False)
        cell = tab[:, 2].reshape(xy, gz, CAP).astype(jnp.int32)
        purk = tab[:, 1].reshape(xy, gz, CAP).astype(jnp.int32)
        brick = jnp.arange(gz, dtype=jnp.int32)[None, :, None]
        row = brick * rows + cell // cols
        place_at = cell % cols + shift * cols - g * chunk + HALO
        sub = jnp.arange(xy, dtype=jnp.int32)[:, None, None] * subs + purk // seg
        return tuple(
            v.reshape(-1) for v in (tab[:, 0].reshape(xy, gz, CAP), row, place_at, sub, purk % seg)
        )

    gain_a, row_a, col_a, sub_a, q_a = side(x, 0)
    go_left = g == 0
    shift = jnp.where(go_left, -1, 1)
    other = x + shift
    near = jnp.logical_and(
        jnp.logical_or(go_left, g == gz - 1), jnp.logical_and(other >= 0, other < xy)
    )
    gain_b, row_b, col_b, sub_b, q_b = side(jnp.clip(other, 0, xy - 1), shift)
    gain_b = jnp.where(near, gain_b, 0.0)
    gain = jnp.concatenate([gain_a, gain_b])
    place_at = jnp.concatenate([col_a, col_b])
    number = jnp.arange(2 * per_s, dtype=jnp.int32)
    inside = jnp.logical_and(place_at >= HALO, place_at < HALO + chunk)
    sent = jnp.where(jnp.logical_and(inside, number < per_s), number, -1)
    fields = jnp.stack(
        [gain]
        + [
            v.astype(F32)
            for v in (
                jnp.concatenate([row_a, row_b]),
                place_at,
                jnp.concatenate([sub_a, sub_b]),
                jnp.concatenate([q_a, q_b]),
                sent,
            )
        ]
    )
    relevant = jnp.logical_and(
        gain > 0.0, jnp.logical_and(place_at >= 0, place_at < chunk + 2 * HALO)
    )
    until = jnp.cumsum(relevant.astype(jnp.int32))
    count = (until[-1] + LANE - 1) // LANE
    target = jnp.where(relevant, until - 1, -1)
    hot = (target[:, None] == number[None, :]).astype(BF16)
    got = jnp.dot(jnp.concatenate(cut3(fields)), hot, preferred_element_type=F32)
    nfield = fields.shape[0]
    packed_rows = got[:nfield] + got[nfield : 2 * nfield] + got[2 * nfield :]
    packed_cols = packed_rows.T
    alive = number < until[-1]

    def as_int(v):
        return v.astype(jnp.int32)

    gain_c = packed_cols[:, 0:1]
    row_c, col_c, sub_c, q_c, sent_c = (
        jnp.where(alive[:, None], as_int(packed_cols[:, i : i + 1]), -1) for i in range(1, 6)
    )
    row_r, sent_r = (jnp.where(alive, as_int(packed_rows[i]), -1) for i in (1, 5))
    lane = jnp.arange(LANE, dtype=jnp.int32)[None, :]
    wing_at = jnp.where(col_c < HALO, col_c, col_c - chunk)
    wing = jnp.logical_or(
        jnp.logical_and(col_c >= 0, col_c < HALO), col_c >= HALO + chunk
    )
    wing_at = jnp.where(wing, (row_c // rows % 4) * WING + wing_at, -1)
    t = {}
    t["gain_halo"] = jnp.where(wing_at == lane, gain_c, 0.0)
    t["gain_own"] = jnp.where(col_c - HALO == lane, gain_c, 0.0)
    t["q"] = (q_c == lane).astype(F32)
    t["slot_lane"] = (jnp.where(sent_c >= 0, sent_c % LANE, -1) == lane).astype(F32)
    t["row_t"] = (row_c == jnp.arange(total_rows)[None, :]).astype(BF16)
    t["sub"] = (sub_c == jnp.arange(nodes)[None, :]).astype(BF16)
    blocks = 2 * per_s // LANE
    row_b = row_r.reshape(blocks, 1, LANE)
    halo_row = (row_b // rows // 4) * rows + row_b % rows
    t["row"] = jnp.concatenate(
        [
            row_b == jnp.arange(total_rows)[None, :, None],
            jnp.logical_and(row_b >= 0, halo_row == jnp.arange(2 * rows)[None, :, None]),
        ],
        axis=1,
    ).astype(BF16)
    sent_b = sent_r.reshape(blocks, 1, LANE)
    t["slot_row"] = (
        jnp.where(sent_b >= 0, sent_b // LANE, -1) == jnp.arange(16)[None, :, None]
    ).astype(BF16)
    flat_row = jnp.transpose(t["row"], (1, 0, 2)).reshape(total_rows + 2 * rows, -1)
    cell_gain = jnp.concatenate(
        [
            hot_dot(flat_row[:total_rows], t["gain_own"]).reshape(gz, rows, LANE),
            hot_dot(flat_row[total_rows:], t["gain_halo"]).reshape(2, rows, LANE),
        ]
    )

    def by_block(v):
        return v.reshape(blocks, LANE, v.shape[-1])

    blk_f = jnp.stack(
        [by_block(t[n]) for n in ("gain_halo", "gain_own", "q", "slot_lane")], axis=1
    )
    blk_s = by_block(t["sub"])
    row_t = jnp.pad(by_block(t["row_t"]), ((0, 0), (0, 0), (0, LANE - total_rows)))
    blk_r = jnp.concatenate([row_t, t["row"], t["slot_row"]], axis=1)

    gain_p = tabs[:, 0].reshape(4, 4, 4, LANE)
    gain_t = jnp.transpose(gain_p, (2, 1, 0, 3))
    gain_t = jnp.concatenate([gain_t, gain_t], axis=2)
    node_p = tabs[:, 1].reshape(xy, per_s).astype(jnp.int32)
    sub_p = (node_p // seg).reshape(xy, 4, 1, LANE)
    hot_sub_p = (sub_p == jnp.arange(subs, dtype=jnp.int32)[None, None, :, None]).astype(BF16)
    hot_q_p = ((node_p % seg)[:, :, None] == jnp.arange(seg)[None, None, :]).astype(BF16)
    tree = {"couple": pcoup}
    tree["node_gain"] = pl.pallas_call(
        node_gain_kernel,
        out_shape=shape(nodes, seg),
        scratch_shapes=[pltpu.VMEM((2, nodes, seg), F32)],
        name="node_gain",
    )(gain_t, hot_sub_p, hot_q_p)
    all_ids = jnp.arange(nodes, dtype=jnp.int32)
    parent_hot = (all_ids[None, :] == parent[:, None]).astype(BF16)
    child_hot = (parent[None, :] == all_ids[:, None]).astype(BF16)
    tree["family"] = jnp.concatenate([parent_hot, child_hot])
    children = jnp.sum(child_hot.astype(F32), axis=1, keepdims=True)
    is_root = (parent < 0).astype(F32)[:, None]
    tree["kinds"] = jnp.where(lane == 0, is_root, jnp.where(lane == seg - 1, children, 0.0))

    par = jnp.stack(
        [
            0.5 * gate_slope,
            0.5 * gate_slope * gate_half,
            jnp.exp(-gate_rate),
            -0.5 * jnp.expm1(-gate_rate),
            conductance,
            conductance * reversal,
        ]
    )
    flags = jnp.stack(
        [
            jnp.logical_and(x == 0, g == 0).astype(jnp.int32),
            jnp.logical_and(x == xy - 1, g == gz - 1).astype(jnp.int32),
            count.astype(jnp.int32),
        ]
    )
    blks, tree, gain_t, hot_sub_p, hot_q_p, cell_gain = lax.optimization_barrier(
        ([blk_f, blk_s, blk_r], [tree[n] for n in TREE], gain_t, hot_sub_p, hot_q_p, cell_gain)
    )
    node_shape = shape(nodes, seg)
    msg_shape = shape(gz * xy, 8, LANE)
    parts = pltpu.VMEM((nodes, 2 * LANE), BF16)
    drawn = pltpu.VMEM((2, nodes, seg), F32)
    send_buf = pltpu.VMEM((16, 8, LANE), F32)
    dma = pltpu.SemaphoreType.DMA
    solver = [gu, gw, ginv, cell_gain]
    limit = pltpu.CompilerParams(vmem_limit_bytes=24 << 20)

    def gate_call(mem, gate):
        return pl.pallas_call(
            gate_kernel,
            out_shape=(gate_shape, slab_shape),
            in_specs=[SMEM, SMEM, VMEM, VMEM, VMEM],
            out_specs=(VMEM, VMEM),
            input_output_aliases={4: 0},
            compiler_params=limit,
            cost_estimate=pl.CostEstimate(flops=8_000_000, transcendentals=900_000, bytes_accessed=3_400_000),
            name="gate",
        )(par, flags, mem, cy, gate)

    def exchange(msg):
        got = lax.all_to_all(msg, ("gz", "xy"), 0, 0, tiled=True)
        return got.reshape(gz, xy, 8, LANE)

    def step_call(final, recv, mem, source, purk, rec, gate):
        args = [flags, par, gain_t, mem, source] + solver + [cy]
        args += [recv, hot_sub_p, hot_q_p, purk, rec] + tree + blks
        specs = [SMEM, SMEM] + [VMEM] * 8 + [ANY] * 12
        outs = [slab_shape, node_shape, node_shape]
        out_specs = [VMEM, ANY, ANY]
        alias = {3: 0, 13: 1, 14: 2}
        scratch = [
            pltpu.VMEM(recv.shape, F32),
            pltpu.VMEM(hot_sub_p.shape, BF16),
            pltpu.VMEM(hot_q_p.shape, BF16),
            pltpu.VMEM((nodes, seg), F32),
            pltpu.VMEM((nodes, seg), F32),
            pltpu.VMEM((2 * nodes, nodes), BF16),
        ]
        scratch += [pltpu.VMEM((nodes, seg), F32)] * 3 + BLOCK_VMEM
        scratch += [parts, drawn, dma((12,)), dma((3, 8))]
        if not final:
            args += [gate]
            specs += [ANY]
            outs += [gate_shape, msg_shape]
            out_specs += [ANY, ANY]
            alias[22] = 3
            scratch += [pltpu.VMEM((nb, nvar, rows, LANE), F32), send_buf, dma((8,)), dma((5,))]
        return pl.pallas_call(
            lambda *refs: step_kernel(final, *refs),
            out_shape=tuple(outs),
            in_specs=specs,
            out_specs=tuple(out_specs),
            scratch_shapes=scratch,
            input_output_aliases=alias,
            compiler_params=limit,
            name="last" if final else "step",
        )(*args)

    gate, source = gate_call(mem, gate)
    mem, msg = pl.pallas_call(
        first_kernel,
        out_shape=(slab_shape, msg_shape),
        in_specs=[SMEM] + [VMEM] * 7 + [ANY] * 3,
        out_specs=(VMEM, ANY),
        scratch_shapes=[parts] + BLOCK_VMEM + [send_buf, dma((3, 8)), dma((8,))],
        compiler_params=limit,
        name="first",
    )(flags, mem, source, purk0, *solver, *blks)

    def two(k, state):
        mem, gate, purk, rec, msg = state
        recv = exchange(msg)
        gate, source = gate_call(mem, gate)
        mem, purk, rec, gate, msg = step_call(False, recv, mem, source, purk, rec, gate)
        return mem, gate, purk, rec, msg

    mem, gate, purk, rec, msg = lax.fori_loop(
        0, STEPS // 2 - 1, two, (mem, gate, purk0, rec0, msg)
    )
    recv = exchange(msg)
    gate, source = gate_call(mem, gate)

    mem, purk, rec = step_call(True, recv, mem, source, purk, rec, gate)

    back = jnp.concatenate([gate[:gz], mem[:gz, None]], axis=1).reshape(gz, -1, chunk)
    back = lax.all_to_all(back, "gz", 0, 0, tiled=True)
    back = back.reshape(gz, nvar + 1, rows, chunk)
    back = jnp.transpose(back, (1, 2, 0, 3)).reshape(nvar + 1, rows, cols)
    purk_mine = lax.dynamic_slice_in_dim(purk, x * subs, subs, axis=0)
    rec_mine = lax.dynamic_slice_in_dim(rec, x * subs, subs, axis=0)
    return back[nvar], back[:nvar], purk_mine, rec_mine


def solution(mesh):
    return jax.shard_map(
        on_device,
        mesh=mesh,
        in_specs=(
            P("gz", "xy"),
            P(None, "gz", "xy"),
            P("gz", "xy"),
            P("gz", "xy"),
            P(),
            P(),
            P(),
            P(),
            P(),
            P("xy", None),
            P("xy", None),
            P("xy", None),
            P(),
            P("xy"),
            P("xy"),
            P("xy", None),
            P("xy"),
        ),
        out_specs=(P("gz", "xy"), P(None, "gz", "xy"), P("xy", None), P("xy", None)),
        check_vma=False,
    )
```

```python
import jax
import jax.numpy as jnp
from jax import lax
from jax.experimental import pallas as pl
from jax.experimental.pallas import tpu as pltpu
from jax.sharding import PartitionSpec as P

STEPS = 16
HALO = 16
CAP = 4
OWN = 8
BRICK = 8
LANE = 128
WING = 32
ROWS_AT = 128
F32 = jnp.float32
BF16 = jnp.bfloat16


def split3(value):
    high = value.astype(BF16)
    rest = value - high.astype(F32)
    mid = rest.astype(BF16)
    low = (rest - mid.astype(F32)).astype(BF16)
    return high, mid, low


def cut3(value):
    high = lax.reduce_precision(value, 8, 7)
    rest = value - high
    mid = lax.reduce_precision(rest, 8, 7)
    return high.astype(BF16), mid.astype(BF16), (rest - mid).astype(BF16)


def hot_dot(hot, value):
    parts = jnp.concatenate(cut3(value), axis=-1)
    got = jnp.dot(hot, parts, preferred_element_type=F32)
    n = value.shape[-1]
    return got[..., :n] + got[..., n : 2 * n] + got[..., 2 * n :]


def table_kernel(field_ref, volt_ref, rec_ref, couple_ref, out_ref):
    fields = field_ref[...]
    nj = fields.shape[1]
    xy = out_ref.shape[0]
    own_row = fields[3:4, :]
    first = lax.broadcasted_iota(jnp.int32, (nj, nj), 0)
    second = lax.broadcasted_iota(jnp.int32, (nj, nj), 1)
    own_col = jnp.sum(jnp.where(first == second, own_row, 0.0), axis=1, keepdims=True)
    earlier = jnp.logical_and(own_col == own_row, first < second)
    rank = jnp.sum(jnp.where(earlier, 1.0, 0.0), axis=0, keepdims=True)
    high = jnp.floor(own_row * (1.0 / xy))
    slot = (own_row - high * xy) * (OWN * CAP) + high * CAP + rank
    slots = xy * OWN * CAP
    at = lax.broadcasted_iota(jnp.int32, (slots, nj), 0)
    hot = jnp.where(at == slot.astype(jnp.int32), 1.0, 0.0).astype(BF16)
    parts = jnp.concatenate([v.astype(F32) for v in split3(fields)], axis=0).astype(BF16)
    got = lax.dot_general(parts, hot, (((1,), (1,)), ((), ())), preferred_element_type=F32)
    n = fields.shape[0]
    got = got[:n] + got[n : 2 * n] + got[2 * n :]
    subs = volt_ref.shape[0]
    span = slots // LANE
    rows = [got[f : f + 1, k * LANE : (k + 1) * LANE] for f in range(3) for k in range(span)]
    for i in range(xy):
        out_ref[i, :subs, :] = volt_ref[...]
        out_ref[i, subs : 2 * subs, :] = rec_ref[...]
        out_ref[i, 2 * subs : 3 * subs, :] = couple_ref[...]
        for r, row in enumerate(rows):
            out_ref[i, 3 * subs + r : 3 * subs + r + 1, :] = row


def pack_kernel(gate_ref, volt_ref, cx_ref, cy_ref, left_ref, right_ref, out_ref):
    lane = lanes()
    nvar = gate_ref.shape[0]
    fields = nvar + 3
    chunks = out_ref.shape[0]
    extra = (volt_ref, cx_ref, cy_ref)
    span = [slice(g * LANE, (g + 1) * LANE) for g in range(chunks)]

    def put(f4, pick, count):
        for fl in range(count):
            at = pl.ds(pl.multiple_of((f4 * 4 + fl) * BRICK, BRICK), BRICK)
            for g in range(chunks):
                out_ref[g, at, :] = pick(fl, g)
        at = pl.ds(pl.multiple_of((fields + f4) * BRICK, BRICK), BRICK)
        for g in range(chunks):
            v = jnp.zeros((BRICK, LANE), F32)
            for fl in range(count):
                base = fl * WING
                low = pltpu.roll(pick(fl, g - 1), (base + HALO) % LANE, 1)
                high = pltpu.roll(pick(fl, g + 1), (base + HALO) % LANE, 1)
                v = jnp.where(jnp.logical_and(lane >= base, lane < base + HALO), low, v)
                v = jnp.where(jnp.logical_and(lane >= base + HALO, lane < base + WING), high, v)
            out_ref[g, at, :] = v

    def body(f4, carried):
        def pick(fl, g):
            f = f4 * 4 + fl
            if g < 0:
                return left_ref[f]
            return right_ref[f] if g == chunks else gate_ref[f, :, span[g]]

        put(f4, pick, 4)
        return carried

    lax.fori_loop(0, nvar // 4, body, 0)

    def pick(fl, g):
        if g < 0:
            return left_ref[nvar + fl]
        return right_ref[nvar + fl] if g == chunks else extra[fl][:, span[g]]

    put(nvar // 4, pick, 3)


def unpack_kernel(in_ref, gate_ref, mem_ref, cy_ref, u_ref, w_ref, ic_ref, near, u_far, w_far, i_far):
    nvar = gate_ref.shape[1]
    fields = nvar + 3
    group = lanes() // WING
    total = OWN * BRICK

    def gather(piece, h, fl):
        v = None
        for lg in range(4):
            part = piece(h * 4 + lg)
            if lg != fl:
                part = pltpu.roll(part, ((lg - fl) * WING) % LANE, 1)
            v = part if v is None else jnp.where(group == lg, part, v)
        return v

    def body(f4, carried):
        at = pl.ds(pl.multiple_of((fields + f4) * BRICK, BRICK), BRICK)
        for fl in range(4):
            f = f4 * 4 + fl
            own = pl.ds(pl.multiple_of(f * BRICK, BRICK), BRICK)
            for b in range(OWN):
                gate_ref[b, f] = in_ref[b, own, :]
            for h in range(2):
                gate_ref[OWN + h, f] = gather(lambda b: in_ref[b, at, :], h, fl)
        return carried

    lax.fori_loop(0, nvar // 4, body, 0)
    tail = slice((fields + nvar // 4) * BRICK, (fields + nvar // 4 + 1) * BRICK)
    for b in range(OWN):
        mem_ref[b] = in_ref[b, nvar * BRICK : (nvar + 1) * BRICK, :]
        cy_ref[b] = in_ref[b, (nvar + 2) * BRICK : (nvar + 3) * BRICK, :]
        c = in_ref[b, (nvar + 1) * BRICK : (nvar + 2) * BRICK, :]
        inv = 1.0 / c
        ic_ref[b] = inv
        near[b * BRICK : (b + 1) * BRICK, :] = inv
        c = in_ref[b, tail, :]
        i_far[b * BRICK : (b + 1) * BRICK, :] = 1.0 / jnp.where(c > 1.0, c, 300.0)
    for h in range(2):
        mem_ref[OWN + h] = gather(lambda b: in_ref[b, tail, :], h, 0)
        cy_ref[OWN + h] = gather(lambda b: in_ref[b, tail, :], h, 2)

    def put_u(i, one, two):
        u_ref[i // BRICK, i % BRICK : i % BRICK + 1, :] = one
        u_far[i : i + 1, :] = two

    def put_w(i, one, two):
        w_ref[i // BRICK, i % BRICK : i % BRICK + 1, :] = one
        w_far[i : i + 1, :] = two

    def both(i):
        return near[i : i + 1, :], i_far[i : i + 1, :]

    u = [jnp.ones((1, LANE), F32)] * 2
    d = [jnp.zeros((1, LANE), F32)] * 2
    put_u(0, *u)
    for i in range(total - 1):
        inv = both(i)
        d = [d[n] + u[n] * inv[n] for n in range(2)]
        u = [u[n] + d[n] for n in range(2)]
        put_u(i + 1, *u)
    inv = both(total - 1)
    e = list(inv)
    scale = [1.0 / (d[n] * (1.0 + e[n]) + (u[n] - d[n]) * e[n]) for n in range(2)]
    w = [jnp.ones((1, LANE), F32)] * 2
    put_w(total - 1, *(w[n] * scale[n] for n in range(2)))
    w = [w[n] + e[n] for n in range(2)]
    put_w(total - 2, *(w[n] * scale[n] for n in range(2)))
    for i in range(total - 2, 0, -1):
        inv = both(i)
        e = [e[n] + w[n] * inv[n] for n in range(2)]
        w = [w[n] + e[n] for n in range(2)]
        put_w(i - 1, *(w[n] * scale[n] for n in range(2)))
    for far, out_ref in ((u_far, u_ref), (w_far, w_ref), (i_far, ic_ref)):
        for h in range(2):
            out_ref[OWN + h] = gather(lambda b: far[b * BRICK : (b + 1) * BRICK, :], h, 1)


def lanes():
    return lax.broadcasted_iota(jnp.int32, (BRICK, LANE), 1)


def sublanes():
    return lax.broadcasted_iota(jnp.int32, (BRICK, LANE), 0)


def wide2(value):
    high = value.astype(BF16)
    return jnp.concatenate([high, (value - high.astype(F32)).astype(BF16)], axis=1)


def fold2(value):
    return value[:, :LANE] + value[:, LANE:]


def neighbours(m, at_left, at_right):
    lane = lanes()
    c = lane % WING
    left, right = [], []
    for b in range(OWN):
        h, base = OWN + b // 4, (b % 4) * WING
        edge = pltpu.roll(m[h], (LANE - (base + HALO - 1)) % LANE, 1)
        edge = jnp.where(at_left, m[b], edge)
        left.append(jnp.where(lane == 0, edge, pltpu.roll(m[b], 1, 1)))
        edge = pltpu.roll(m[h], (LANE - 1 - (base + HALO)) % LANE, 1)
        edge = jnp.where(at_right, m[b], edge)
        right.append(jnp.where(lane == LANE - 1, edge, pltpu.roll(m[b], LANE - 1, 1)))
    for h in range(2):
        v = m[OWN + h]
        lf = jnp.where(c == 0, v, pltpu.roll(v, 1, 1))
        rt = jnp.where(c == WING - 1, v, pltpu.roll(v, LANE - 1, 1))
        for k in range(4):
            own, base = m[h * 4 + k], k * WING
            lf = jnp.where(lane == base + HALO, pltpu.roll(own, (base + HALO + 1) % LANE, 1), lf)
            rt = jnp.where(lane == base + HALO - 1, pltpu.roll(own, (base + HALO - 1) % LANE, 1), rt)
        left.append(lf)
        right.append(rt)
    return left, right


def gate_step(m, par_ref, flag_ref, cy_ref, gate_in, gate_out):
    zero = jnp.zeros((BRICK, LANE), F32)
    nb = OWN + 2

    def body(k, carried):
        total, push = carried
        slope, offset, decay = par_ref[0, k], par_ref[1, k], par_ref[2, k]
        grow, weight, driven = par_ref[3, k], par_ref[4, k], par_ref[5, k]
        total_next, push_next = [], []
        for b in range(nb):
            bend = jnp.tanh(m[b] * slope - offset)
            gate = (gate_in[b, k] * decay + grow) + grow * bend
            gate_out[b, k] = gate
            total_next.append(total[b] + weight * gate)
            push_next.append(push[b] + driven * gate)
        return tuple(total_next), tuple(push_next)

    start = (tuple([zero] * nb), tuple([zero] * nb))
    total, push = lax.fori_loop(0, gate_in.shape[1], body, start, unroll=8)
    left, right = neighbours(m, flag_ref[0] > 0, flag_ref[1] > 0)
    return [
        m[b] - (m[b] * total[b] - push[b]) + cy_ref[b] * (left[b] + right[b] - 2.0 * m[b])
        for b in range(nb)
    ]


def solve(source, u_ref, w_ref, ic_ref):
    row, lane = sublanes(), lanes()
    nb = OWN + 2
    before, after, total_b, total_a = [], [], [], []
    for b in range(nb):
        s = source[b] * ic_ref[b]
        p = u_ref[b] * s
        q = w_ref[b] * s
        for step in (1, 2, 4):
            p = p + jnp.where(row >= step, pltpu.roll(p, step, 0), 0.0)
            q = q + jnp.where(row < BRICK - step, pltpu.roll(q, BRICK - step, 0), 0.0)
        total_b.append(jnp.broadcast_to(p[BRICK - 1 : BRICK, :], p.shape))
        total_a.append(jnp.broadcast_to(q[0:1, :], q.shape))
        before.append(p)
        after.append(jnp.where(row < BRICK - 1, pltpu.roll(q, BRICK - 1, 0), 0.0))
    run = None
    for b in range(OWN):
        if run is not None:
            before[b] = before[b] + run
        run = total_b[b] if run is None else run + total_b[b]
    run = None
    for b in range(OWN - 1, -1, -1):
        if run is not None:
            after[b] = after[b] + run
        run = total_a[b] if run is None else run + total_a[b]

    def scan4(t, up):
        shift = (lambda v, n: pltpu.roll(v, n, 1)) if up else (lambda v, n: pltpu.roll(v, LANE - n, 1))
        ok = (lambda n: lane >= n) if up else (lambda n: lane < LANE - n)
        one = t + jnp.where(ok(WING), shift(t, WING), 0.0)
        two = one + jnp.where(ok(2 * WING), shift(one, 2 * WING), 0.0)
        return jnp.where(ok(WING), shift(two, WING), 0.0)

    def all4(t):
        two = t + pltpu.roll(t, WING, 1)
        return two + pltpu.roll(two, 2 * WING, 1)

    before[OWN] = before[OWN] + scan4(total_b[OWN], True)
    before[OWN + 1] = before[OWN + 1] + scan4(total_b[OWN + 1], True) + all4(total_b[OWN])
    after[OWN + 1] = after[OWN + 1] + scan4(total_a[OWN + 1], False)
    after[OWN] = after[OWN] + scan4(total_a[OWN], False) + all4(total_a[OWN + 1])
    return [w_ref[b] * before[b] + u_ref[b] * after[b] for b in range(nb)]


def over_blocks(count, blk, use, start):
    def body(b, carried):
        return use(blk["f0"].at[b], blk["s0"].at[b], blk["r0"].at[b], carried)

    return lax.fori_loop(0, count, body, start)


def block_copies(b, blk, sem):
    return [
        pltpu.make_async_copy(blk[n].at[b], blk[n + "0"].at[b], sem.at[k, b])
        for k, n in enumerate("fsr")
    ]


def start_blocks(count, blk, sem):
    def body(b, carried):
        for copy in block_copies(b, blk, sem):
            copy.start()
        return carried

    lax.fori_loop(0, count, body, 0)


def wait_blocks(count, blk, sem):
    def body(b, carried):
        for copy in block_copies(b, blk, sem):
            copy.wait()
        return carried

    lax.fori_loop(0, count, body, 0)


def sample(m, count, blk):
    rows = jnp.concatenate(m[:OWN], axis=0)
    big = wide2(jnp.concatenate([rows, jnp.zeros_like(rows)], axis=0))

    def use(f, s, r, msg):
        picked = fold2(jnp.dot(r[:LANE, :], big, preferred_element_type=F32))
        picked = jnp.where(f[1] > 0.0, picked, 0.0)
        value = jnp.sum(picked, axis=1, keepdims=True)
        value = wide2(value * f[3])
        slot_row = r[ROWS_AT + 10 * BRICK : ROWS_AT + 12 * BRICK, :]
        return msg + fold2(jnp.dot(slot_row, value, preferred_element_type=F32))

    return over_blocks(count, blk, use, jnp.zeros((2 * BRICK, LANE), F32))


def send(early, late, buf, msg_out, sem):
    both = jnp.concatenate([early[:4], late[:4]], axis=0)
    n = buf.shape[0]
    for i in range(n):
        buf[i] = both
    copies = [
        pltpu.make_async_copy(buf, msg_out.at[pl.ds(i * n, n)], sem.at[i])
        for i in range(msg_out.shape[0] // n)
    ]
    for copy in copies:
        copy.start()
    return copies


def inject(m, count, purk_parts, cell_gain, blk):
    nr = OWN * BRICK

    def use(f, s, r, carried):
        own, halo = carried
        got = fold2(jnp.dot(s[...], purk_parts[...], preferred_element_type=F32))
        volts = jnp.sum(got * f[2], axis=1, keepdims=True)
        own = own + fold2(
            jnp.dot(r[ROWS_AT : ROWS_AT + nr, :], wide2(volts * f[1]), preferred_element_type=F32)
        )
        halo = halo + fold2(
            jnp.dot(
                r[ROWS_AT + nr : ROWS_AT + nr + 2 * BRICK, :],
                wide2(volts * f[0]),
                preferred_element_type=F32,
            )
        )
        return own, halo

    start = (jnp.zeros((nr, LANE), F32), jnp.zeros((2 * BRICK, LANE), F32))
    own, halo = over_blocks(count, blk, use, start)
    parts = [own[b * BRICK : (b + 1) * BRICK] for b in range(OWN)]
    parts += [halo[:BRICK], halo[BRICK:]]
    return [parts[b] - cell_gain[b] * m[b] for b in range(OWN + 2)]


def to_nodes(tile, hot_sub, hot_q, out_ref, waits=()):
    subs = hot_sub.shape[2]
    for s in range(hot_q.shape[0]):
        if waits and s % 4 == 0:
            waits[s // 4].wait()
        rows = []
        for time in range(2):
            high, low = [], []
            for xh in range(4):
                r = tile[xh][s % 4][time * 4 + s // 4 : time * 4 + s // 4 + 1, :]
                hot = hot_sub[s, xh]
                up = r.astype(BF16).astype(F32)
                high.append(hot * jnp.broadcast_to(up, (subs, LANE)).astype(BF16))
                low.append(hot * jnp.broadcast_to(r - up, (subs, LANE)).astype(BF16))
            rows += [jnp.concatenate(high, axis=1), jnp.concatenate(low, axis=1)]
        got = jnp.dot(jnp.concatenate(rows, axis=0), hot_q[s], preferred_element_type=F32)
        out_ref[0, s * subs : (s + 1) * subs, :] = got[:subs] + got[subs : 2 * subs]
        out_ref[1, s * subs : (s + 1) * subs, :] = got[2 * subs : 3 * subs] + got[3 * subs :]


def node_gain_kernel(gain_ref, hot_sub, hot_q, out_ref, both):
    tile = [[gain_ref[xh, a] for a in range(4)] for xh in range(4)]
    to_nodes(tile, hot_sub, hot_q, both)
    out_ref[...] = both[0]


def arrange(recv_ref, gain_ref):
    group = lanes() // WING
    summed = []
    for x in range(recv_ref.shape[1]):
        v = recv_ref[0, x]
        for g in range(1, recv_ref.shape[0]):
            v = v + recv_ref[g, x]
        summed.append(v)
    tile = []
    for xh in range(4):
        row = []
        for a in range(4):
            v = None
            for b in range(4):
                piece = summed[xh * 4 + b]
                if a != b:
                    piece = pltpu.roll(piece, ((b - a) * WING) % LANE, 1)
                v = piece if v is None else jnp.where(group == b, piece, v)
            row.append(v * gain_ref[xh, a])
        tile.append(row)
    return tile


def purk_step(purk, rec, drawn, t):
    nodes = purk.shape[0]
    lane = lax.broadcasted_iota(jnp.int32, purk.shape, 1)
    high, mid, low = (v.astype(F32) for v in split3(purk))
    last = LANE - 1
    ends = jnp.where(lane == last, high, 0.0) + jnp.where(lane == 0, high, 0.0)
    ends = jnp.where(lane == last - 1, pltpu.roll(mid, last, 1), ends)
    ends = jnp.where(lane == last - 2, pltpu.roll(low, last - 1, 1), ends)
    ends = jnp.where(lane == 1, pltpu.roll(mid, 1, 1), ends)
    ends = jnp.where(lane == 2, pltpu.roll(low, 2, 1), ends)
    kin = jnp.dot(t["family"][...], ends.astype(BF16), preferred_element_type=F32)
    up, down = kin[:nodes], kin[nodes:]
    up = up + pltpu.roll(up, 1, 1) + pltpu.roll(up, 2, 1)
    down = down + pltpu.roll(down, last, 1) + pltpu.roll(down, last - 1, 1)
    left = pltpu.roll(jnp.where(lane == last, up, purk), 1, 1)
    kinds = t["kinds"][...]
    left = jnp.where(jnp.logical_and(lane == 0, kinds > 0.0), purk, left)
    right = jnp.where(lane == last, purk, pltpu.roll(purk, last, 1))
    spread = left + right - 2.0 * purk
    extra = pltpu.roll(down, last, 1) - kinds * purk
    spread = spread + jnp.where(lane == last, extra, 0.0)
    purk_next = (
        purk
        + t["couple"][...] * spread
        + 0.2 * purk * (purk - 0.15) * (1.0 - purk)
        - 0.1 * rec
        - (t["node_gain"][...] * purk - drawn)
    )
    return purk_next, rec + 0.05 * (purk - 0.5 * rec)


TREE = ("family", "couple", "node_gain", "kinds")
BLOCK_VMEM = [
    pltpu.VMEM((8, 4, LANE, LANE), F32),
    pltpu.VMEM((8, LANE, 4 * LANE), BF16),
    pltpu.VMEM((8, ROWS_AT + 12 * BRICK, LANE), BF16),
]


def block_refs(hbm, vmem):
    blk = dict(zip("fsr", hbm))
    blk.update(zip(("f0", "s0", "r0"), vmem))
    return blk


def gate_kernel(par_ref, flag_ref, mem_ref, cy_ref, gate_ref, gate_out, source_out):
    m = [mem_ref[b] for b in range(OWN + 2)]
    source = gate_step(m, par_ref, flag_ref, cy_ref, gate_ref, gate_out)
    for b in range(OWN + 2):
        source_out[b] = source[b]


def first_kernel(
    flag_ref, mem_ref, source_ref, purk_ref, u_ref, w_ref, ic_ref, cg_ref, f_hbm, s_hbm, r_hbm,
    mem_out, msg_out, parts, f0, s0, r0, buf, sem1, sem2,
):
    nb = OWN + 2
    count = flag_ref[2]
    blk = block_refs((f_hbm, s_hbm, r_hbm), (f0, s0, r0))
    start_blocks(count, blk, sem1)
    parts[...] = wide2(purk_ref[...])
    m = [mem_ref[b] for b in range(nb)]
    wait_blocks(count, blk, sem1)
    early = sample(m, count, blk)
    add = inject(m, count, parts, cg_ref, blk)
    m = solve([source_ref[b] + add[b] for b in range(nb)], u_ref, w_ref, ic_ref)
    for b in range(nb):
        mem_out[b] = m[b]
    for copy in send(early, sample(m, count, blk), buf, msg_out, sem2):
        copy.wait()


def step_kernel(final, *refs):
    flag_ref, par_ref, gain_ref, mem_ref, source_ref, u_ref, w_ref, ic_ref, cg_ref, cy_ref = refs[:10]
    recv_hbm, sub_hbm, q_hbm, purk_hbm, rec_hbm = refs[10:15]
    tree_hbm = refs[15:19]
    blk_hbm = refs[19:22]
    rest = refs[22:]
    if final:
        mem_out, purk_out, rec_out = rest[:3]
        rest = rest[3:]
    else:
        gate_hbm, mem_out, purk_out, rec_out, gate_out, msg_out = rest[:6]
        rest = rest[6:]
    recv, hot_sub, hot_q, purk_buf, rec_buf, family, couple, node_gain, kinds = rest[:9]
    f0, s0, r0, parts, drawn, sem, sem1 = rest[9:16]
    if not final:
        gates, buf, sem2, sem3 = rest[16:]
    nb = OWN + 2
    count = flag_ref[2]
    blk = block_refs(blk_hbm, (f0, s0, r0))
    t = dict(zip(TREE, (family, couple, node_gain, kinds)))
    plan = [(recv_hbm, recv), (sub_hbm, hot_sub)]
    quarter = hot_q.shape[0] // 4
    for i in range(4):
        cut = pl.ds(i * quarter, quarter)
        plan.append((q_hbm.at[cut], hot_q.at[cut]))
    plan += [(purk_hbm, purk_buf), (rec_hbm, rec_buf)]
    plan += list(zip(tree_hbm, (family, couple, node_gain, kinds)))
    loads = [pltpu.make_async_copy(a, b, sem.at[k]) for k, (a, b) in enumerate(plan)]
    for load in loads:
        load.start()
    start_blocks(count, blk, sem1)
    gate_loads = []
    if not final:
        for i in range(nb // 2):
            cut = pl.ds(2 * i, 2)
            gate_loads.append(pltpu.make_async_copy(gate_hbm.at[cut], gates.at[cut], sem3.at[i]))
        for load in gate_loads:
            load.start()
    for load in loads[:2]:
        load.wait()
    to_nodes(arrange(recv, gain_ref), hot_sub, hot_q, drawn, loads[2:6])
    m = [mem_ref[b] for b in range(nb)]
    for load in loads[6:]:
        load.wait()
    wait_blocks(count, blk, sem1)
    purk = purk_buf[...] + drawn[0]
    purk_buf[...] = purk
    parts[...] = wide2(purk)
    add = inject(m, count, parts, cg_ref, blk)
    m = solve([source_ref[b] + add[b] for b in range(nb)], u_ref, w_ref, ic_ref)
    purk, rec = purk_step(purk_buf[...], rec_buf[...], drawn[1], t)
    purk_buf[...] = purk
    rec_buf[...] = rec
    stores = [
        pltpu.make_async_copy(purk_buf, purk_out, sem.at[0]),
        pltpu.make_async_copy(rec_buf, rec_out, sem.at[1]),
    ]
    for store in stores:
        store.start()
    if not final:
        parts[...] = wide2(purk)
        for load in gate_loads:
            load.wait()
        source = gate_step(m, par_ref, flag_ref, cy_ref, gates, gates)
        for i in range(nb // 2):
            cut = pl.ds(2 * i, 2)
            store = pltpu.make_async_copy(gates.at[cut], gate_out.at[cut], sem3.at[i])
            store.start()
            stores.append(store)
        early = sample(m, count, blk)
        add = inject(m, count, parts, cg_ref, blk)
        m = solve([source[b] + add[b] for b in range(nb)], u_ref, w_ref, ic_ref)
        stores += send(early, sample(m, count, blk), buf, msg_out, sem2)
    for b in range(nb):
        mem_out[b] = m[b]
    for store in stores:
        store.wait()


def drift_kernel(
    par_ref, flag_ref, mem_ref, cy_ref, gate_ref, purk_ref, rec_ref, family, couple, node_gain,
    kinds, gate_out, source_out, purk_out, rec_out,
):
    t = dict(zip(TREE, (family, couple, node_gain, kinds)))
    purk, rec = purk_step(purk_ref[...], rec_ref[...], 0.0, t)
    purk_out[...] = purk
    rec_out[...] = rec
    gate_kernel(par_ref, flag_ref, mem_ref, cy_ref, gate_ref, gate_out, source_out)


VMEM = pl.BlockSpec()
ANY = pl.BlockSpec(memory_space=pl.ANY)
SMEM = pl.BlockSpec(memory_space=pltpu.SMEM)


def shape(*dims):
    return jax.ShapeDtypeStruct(dims, F32)


def on_device(
    voltage,
    gates,
    couple_x,
    couple_y,
    gate_half,
    gate_slope,
    gate_rate,
    conductance,
    reversal,
    purk_volt,
    purk_recovery,
    purk_couple,
    parent,
    junc_purk,
    junc_cell,
    junc_owner,
    junc_gain,
):
    rows, cols = voltage.shape
    subs, seg = purk_volt.shape
    gz = lax.axis_size("gz")
    xy = lax.axis_size("xy")
    g = lax.axis_index("gz")
    x = lax.axis_index("xy")
    nvar = gates.shape[0]
    chunk = cols // gz
    wide = chunk + 2 * HALO
    total_rows = rows * gz
    nodes = parent.shape[0]
    nj = junc_gain.shape[0]
    slots = gz * CAP
    per_s = xy * slots

    fields = jnp.stack(
        [junc_gain]
        + [v.astype(F32) for v in (junc_purk, junc_cell, junc_owner[:, 0])]
        + [jnp.zeros_like(junc_gain)] * 4
    )
    mine = pl.pallas_call(
        table_kernel,
        out_shape=shape(xy, 3 * subs + 3 * per_s // seg, seg),
        name="table",
    )(fields, purk_volt, purk_recovery, purk_couple)
    allp = lax.all_to_all(mine, "xy", 0, 0, tiled=True)
    purk0 = allp[:, :subs].reshape(nodes, seg)
    rec0 = allp[:, subs : 2 * subs].reshape(nodes, seg)
    pcoup = allp[:, 2 * subs : 3 * subs].reshape(nodes, seg)
    tabs = allp[:, 3 * subs :].reshape(xy, 3, xy, slots)

    nb = gz + 2
    nf = nvar + 3

    def edge(at):
        cut = slice(at, at + chunk)
        return jnp.concatenate(
            [gates[:, :, cut], voltage[None, :, cut], couple_x[None, :, cut], couple_y[None, :, cut]]
        )

    left = lax.ppermute(edge(cols - chunk), "xy", [(i, i + 1) for i in range(xy - 1)])
    right = lax.ppermute(edge(0), "xy", [(i + 1, i) for i in range(xy - 1)])
    limit = pltpu.CompilerParams(vmem_limit_bytes=16 << 20)
    packed = pl.pallas_call(
        pack_kernel,
        out_shape=shape(gz, (nf + nvar // 4 + 1) * rows, chunk),
        compiler_params=limit,
        name="pack",
    )(gates, voltage, couple_x, couple_y, left, right)
    packed = lax.all_to_all(packed, "gz", 0, 0, tiled=True)
    slab_shape = shape(nb, rows, LANE)
    gate_shape = shape(nb, nvar, rows, LANE)
    flat = pltpu.VMEM((total_rows, LANE), F32)
    gate, mem, cy, gu, gw, ginv = pl.pallas_call(
        unpack_kernel,
        out_shape=(gate_shape,) + (slab_shape,) * 5,
        scratch_shapes=[flat] * 4,
        compiler_params=limit,
        name="unpack",
    )(packed)

    def side(which, shift):
        tab = lax.dynamic_index_in_dim(tabs, which, 2, keepdims=False)
        cell = tab[:, 2].reshape(xy, gz, CAP).astype(jnp.int32)
        purk = tab[:, 1].reshape(xy, gz, CAP).astype(jnp.int32)
        brick = jnp.arange(gz, dtype=jnp.int32)[None, :, None]
        row = brick * rows + cell // cols
        place_at = cell % cols + shift * cols - g * chunk + HALO
        sub = jnp.arange(xy, dtype=jnp.int32)[:, None, None] * subs + purk // seg
        return tuple(
            v.reshape(-1) for v in (tab[:, 0].reshape(xy, gz, CAP), row, place_at, sub, purk % seg)
        )

    gain_a, row_a, col_a, sub_a, q_a = side(x, 0)
    go_left = g == 0
    shift = jnp.where(go_left, -1, 1)
    other = x + shift
    near = jnp.logical_and(
        jnp.logical_or(go_left, g == gz - 1), jnp.logical_and(other >= 0, other < xy)
    )
    gain_b, row_b, col_b, sub_b, q_b = side(jnp.clip(other, 0, xy - 1), shift)
    gain_b = jnp.where(near, gain_b, 0.0)
    gain = jnp.concatenate([gain_a, gain_b])
    place_at = jnp.concatenate([col_a, col_b])
    number = jnp.arange(2 * per_s, dtype=jnp.int32)
    inside = jnp.logical_and(place_at >= HALO, place_at < HALO + chunk)
    sent = jnp.where(jnp.logical_and(inside, number < per_s), number, -1)
    fields = jnp.stack(
        [gain]
        + [
            v.astype(F32)
            for v in (
                jnp.concatenate([row_a, row_b]),
                place_at,
                jnp.concatenate([sub_a, sub_b]),
                jnp.concatenate([q_a, q_b]),
                sent,
            )
        ]
    )
    relevant = jnp.logical_and(
        gain > 0.0, jnp.logical_and(place_at >= 0, place_at < chunk + 2 * HALO)
    )
    until = jnp.cumsum(relevant.astype(jnp.int32))
    count = (until[-1] + LANE - 1) // LANE
    target = jnp.where(relevant, until - 1, -1)
    hot = (target[:, None] == number[None, :]).astype(BF16)
    got = jnp.dot(jnp.concatenate(cut3(fields)), hot, preferred_element_type=F32)
    nfield = fields.shape[0]
    packed_rows = got[:nfield] + got[nfield : 2 * nfield] + got[2 * nfield :]
    packed_cols = packed_rows.T
    alive = number < until[-1]

    def as_int(v):
        return v.astype(jnp.int32)

    gain_c = packed_cols[:, 0:1]
    row_c, col_c, sub_c, q_c, sent_c = (
        jnp.where(alive[:, None], as_int(packed_cols[:, i : i + 1]), -1) for i in range(1, 6)
    )
    row_r, sent_r = (jnp.where(alive, as_int(packed_rows[i]), -1) for i in (1, 5))
    lane = jnp.arange(LANE, dtype=jnp.int32)[None, :]
    wing_at = jnp.where(col_c < HALO, col_c, col_c - chunk)
    wing = jnp.logical_or(
        jnp.logical_and(col_c >= 0, col_c < HALO), col_c >= HALO + chunk
    )
    wing_at = jnp.where(wing, (row_c // rows % 4) * WING + wing_at, -1)
    t = {}
    t["gain_halo"] = jnp.where(wing_at == lane, gain_c, 0.0)
    t["gain_own"] = jnp.where(col_c - HALO == lane, gain_c, 0.0)
    t["q"] = (q_c == lane).astype(F32)
    t["slot_lane"] = (jnp.where(sent_c >= 0, sent_c % LANE, -1) == lane).astype(F32)
    t["row_t"] = (row_c == jnp.arange(total_rows)[None, :]).astype(BF16)
    t["sub"] = (sub_c == jnp.arange(nodes)[None, :]).astype(BF16)
    blocks = 2 * per_s // LANE
    row_b = row_r.reshape(blocks, 1, LANE)
    halo_row = (row_b // rows // 4) * rows + row_b % rows
    t["row"] = jnp.concatenate(
        [
            row_b == jnp.arange(total_rows)[None, :, None],
            jnp.logical_and(row_b >= 0, halo_row == jnp.arange(2 * rows)[None, :, None]),
        ],
        axis=1,
    ).astype(BF16)
    sent_b = sent_r.reshape(blocks, 1, LANE)
    t["slot_row"] = (
        jnp.where(sent_b >= 0, sent_b // LANE, -1) == jnp.arange(16)[None, :, None]
    ).astype(BF16)
    flat_row = jnp.transpose(t["row"], (1, 0, 2)).reshape(total_rows + 2 * rows, -1)
    cell_gain = jnp.concatenate(
        [
            hot_dot(flat_row[:total_rows], t["gain_own"]).reshape(gz, rows, LANE),
            hot_dot(flat_row[total_rows:], t["gain_halo"]).reshape(2, rows, LANE),
        ]
    )

    def by_block(v):
        return v.reshape(blocks, LANE, v.shape[-1])

    blk_f = jnp.stack(
        [by_block(t[n]) for n in ("gain_halo", "gain_own", "q", "slot_lane")], axis=1
    )
    blk_s = by_block(t["sub"])
    row_t = jnp.pad(by_block(t["row_t"]), ((0, 0), (0, 0), (0, LANE - total_rows)))
    blk_r = jnp.concatenate([row_t, t["row"], t["slot_row"]], axis=1)

    gain_p = tabs[:, 0].reshape(4, 4, 4, LANE)
    gain_t = jnp.transpose(gain_p, (2, 1, 0, 3))
    gain_t = jnp.concatenate([gain_t, gain_t], axis=2)
    node_p = tabs[:, 1].reshape(xy, per_s).astype(jnp.int32)
    sub_p = (node_p // seg).reshape(xy, 4, 1, LANE)
    hot_sub_p = (sub_p == jnp.arange(subs, dtype=jnp.int32)[None, None, :, None]).astype(BF16)
    hot_q_p = ((node_p % seg)[:, :, None] == jnp.arange(seg)[None, None, :]).astype(BF16)
    tree = {"couple": pcoup}
    tree["node_gain"] = pl.pallas_call(
        node_gain_kernel,
        out_shape=shape(nodes, seg),
        scratch_shapes=[pltpu.VMEM((2, nodes, seg), F32)],
        name="node_gain",
    )(gain_t, hot_sub_p, hot_q_p)
    all_ids = jnp.arange(nodes, dtype=jnp.int32)
    parent_hot = (all_ids[None, :] == parent[:, None]).astype(BF16)
    child_hot = (parent[None, :] == all_ids[:, None]).astype(BF16)
    tree["family"] = jnp.concatenate([parent_hot, child_hot])
    children = jnp.sum(child_hot.astype(F32), axis=1, keepdims=True)
    is_root = (parent < 0).astype(F32)[:, None]
    tree["kinds"] = jnp.where(lane == 0, is_root, jnp.where(lane == seg - 1, children, 0.0))

    par = jnp.stack(
        [
            0.5 * gate_slope,
            0.5 * gate_slope * gate_half,
            jnp.exp(-gate_rate),
            -0.5 * jnp.expm1(-gate_rate),
            conductance,
            conductance * reversal,
        ]
    )
    flags = jnp.stack(
        [
            jnp.logical_and(x == 0, g == 0).astype(jnp.int32),
            jnp.logical_and(x == xy - 1, g == gz - 1).astype(jnp.int32),
            count.astype(jnp.int32),
        ]
    )
    blks, tree, gain_t, hot_sub_p, hot_q_p, cell_gain = lax.optimization_barrier(
        ([blk_f, blk_s, blk_r], [tree[n] for n in TREE], gain_t, hot_sub_p, hot_q_p, cell_gain)
    )
    node_shape = shape(nodes, seg)
    msg_shape = shape(gz * xy, 8, LANE)
    parts = pltpu.VMEM((nodes, 2 * LANE), BF16)
    drawn = pltpu.VMEM((2, nodes, seg), F32)
    send_buf = pltpu.VMEM((16, 8, LANE), F32)
    dma = pltpu.SemaphoreType.DMA
    solver = [gu, gw, ginv, cell_gain]
    limit = pltpu.CompilerParams(vmem_limit_bytes=24 << 20)

    def gate_call(mem, gate):
        return pl.pallas_call(
            gate_kernel,
            out_shape=(gate_shape, slab_shape),
            in_specs=[SMEM, SMEM, VMEM, VMEM, VMEM],
            out_specs=(VMEM, VMEM),
            input_output_aliases={4: 0},
            compiler_params=limit,
            cost_estimate=pl.CostEstimate(flops=8_000_000, transcendentals=900_000, bytes_accessed=3_400_000),
            name="gate",
        )(par, flags, mem, cy, gate)

    def drift_call(mem, gate, purk, rec):
        return pl.pallas_call(
            drift_kernel,
            out_shape=(gate_shape, slab_shape, node_shape, node_shape),
            in_specs=[SMEM, SMEM] + [VMEM] * 9,
            out_specs=(VMEM,) * 4,
            input_output_aliases={4: 0},
            compiler_params=limit,
            cost_estimate=pl.CostEstimate(flops=8_000_000, transcendentals=900_000, bytes_accessed=3_400_000),
            name="drift",
        )(par, flags, mem, cy, gate, purk, rec, *tree)

    def exchange(msg):
        got = lax.all_to_all(msg, ("gz", "xy"), 0, 0, tiled=True)
        return got.reshape(gz, xy, 8, LANE)

    def step_call(final, recv, mem, source, purk, rec, gate):
        args = [flags, par, gain_t, mem, source] + solver + [cy]
        args += [recv, hot_sub_p, hot_q_p, purk, rec] + tree + blks
        specs = [SMEM, SMEM] + [VMEM] * 8 + [ANY] * 12
        outs = [slab_shape, node_shape, node_shape]
        out_specs = [VMEM, ANY, ANY]
        alias = {3: 0, 13: 1, 14: 2}
        scratch = [
            pltpu.VMEM(recv.shape, F32),
            pltpu.VMEM(hot_sub_p.shape, BF16),
            pltpu.VMEM(hot_q_p.shape, BF16),
            pltpu.VMEM((nodes, seg), F32),
            pltpu.VMEM((nodes, seg), F32),
            pltpu.VMEM((2 * nodes, nodes), BF16),
        ]
        scratch += [pltpu.VMEM((nodes, seg), F32)] * 3 + BLOCK_VMEM
        scratch += [parts, drawn, dma((12,)), dma((3, 8))]
        if not final:
            args += [gate]
            specs += [ANY]
            outs += [gate_shape, msg_shape]
            out_specs += [ANY, ANY]
            alias[22] = 3
            scratch += [pltpu.VMEM((nb, nvar, rows, LANE), F32), send_buf, dma((8,)), dma((5,))]
        return pl.pallas_call(
            lambda *refs: step_kernel(final, *refs),
            out_shape=tuple(outs),
            in_specs=specs,
            out_specs=tuple(out_specs),
            scratch_shapes=scratch,
            input_output_aliases=alias,
            compiler_params=limit,
            name="last" if final else "step",
        )(*args)

    gate, source = gate_call(mem, gate)
    mem, msg = pl.pallas_call(
        first_kernel,
        out_shape=(slab_shape, msg_shape),
        in_specs=[SMEM] + [VMEM] * 7 + [ANY] * 3,
        out_specs=(VMEM, ANY),
        scratch_shapes=[parts] + BLOCK_VMEM + [send_buf, dma((3, 8)), dma((8,))],
        compiler_params=limit,
        name="first",
    )(flags, mem, source, purk0, *solver, *blks)

    def two(k, state):
        mem, gate, purk, rec, msg = state
        recv = exchange(msg)
        gate, source, purk, rec = drift_call(mem, gate, purk, rec)
        mem, purk, rec, gate, msg = step_call(False, recv, mem, source, purk, rec, gate)
        return mem, gate, purk, rec, msg

    mem, gate, purk, rec, msg = lax.fori_loop(
        0, STEPS // 2 - 1, two, (mem, gate, purk0, rec0, msg)
    )
    recv = exchange(msg)
    gate, source, purk, rec = drift_call(mem, gate, purk, rec)

    mem, purk, rec = step_call(True, recv, mem, source, purk, rec, gate)

    back = jnp.concatenate([gate[:gz], mem[:gz, None]], axis=1).reshape(gz, -1, chunk)
    back = lax.all_to_all(back, "gz", 0, 0, tiled=True)
    back = back.reshape(gz, nvar + 1, rows, chunk)
    back = jnp.transpose(back, (1, 2, 0, 3)).reshape(nvar + 1, rows, cols)
    purk_mine = lax.dynamic_slice_in_dim(purk, x * subs, subs, axis=0)
    rec_mine = lax.dynamic_slice_in_dim(rec, x * subs, subs, axis=0)
    return back[nvar], back[:nvar], purk_mine, rec_mine


def solution(mesh):
    return jax.shard_map(
        on_device,
        mesh=mesh,
        in_specs=(
            P("gz", "xy"),
            P(None, "gz", "xy"),
            P("gz", "xy"),
            P("gz", "xy"),
            P(),
            P(),
            P(),
            P(),
            P(),
            P("xy", None),
            P("xy", None),
            P("xy", None),
            P(),
            P("xy"),
            P("xy"),
            P("xy", None),
            P("xy"),
        ),
        out_specs=(P("gz", "xy"), P(None, "gz", "xy"), P("xy", None), P("xy", None)),
        check_vma=False,
    )
```
